512 devices in a mesh: gx: 32 (over z_lo, x), gy: 4 (over y), gz: 4 (over z_hi, core).
Axes of the slice: x: 4, y: 4, z: 16 (z_hi: 2, z_lo: 8; z = z_hi * 8 + z_lo), core: 2. Of those that a mesh axis runs over, the one named last changes fastest.
Arguments:
- populations: float32 [19, 256, 64, 512], P(None, 'gx', 'gy', 'gz'), may hold values from 0.01 to 0.06
- adjoint_next: float32 [19, 256, 64, 512], P(None, 'gx', 'gy', 'gz'), may hold values from -6 to 6
Outputs:
- adjoint_before: float32 [19, 256, 64, 512], P(None, 'gx', 'gy', 'gz')
The draws below stay inside these ranges and needn't reach their ends.
All inputs are finite; a program needn't handle non-finite values.
Results may differ from the reference program's by a relative error of at most 0.00002.
Values sent between devices are 32-bit elements; how exact they have to be, the bound alone decides.
A program may use at most 64 MiB of HBM per device.

```python
import math
import jax
import jax.numpy as jnp
from jax import lax

Q = 19
NX = 256
NY = 64
NZ = 512
N_GX = 32


def block_levels(own_key, shape, pieces, least, high):
    def one(axis_at, parts):
        steps = jax.random.uniform(jax.random.fold_in(jax.random.fold_in(own_key, 6), axis_at), (parts,), jnp.float32, least / len(pieces), high / len(pieces))
        return jnp.repeat(jnp.exp(steps), shape[axis_at] // parts).reshape((-1,) + (1,) * (len(shape) - axis_at - 1))

    level = one(*pieces[0])
    for cut in pieces[1:]:
        level = level * one(*cut)
    return level


def gaussian(rng, dims, deviation, bound, split=(), held_as=jnp.bfloat16):
    drawn = jax.random.normal(rng, dims, jnp.float32) * deviation
    if len(split) > 0:
        drawn = block_levels(rng, dims, split, -0.22, 0.18) * drawn
    return jnp.clip(drawn, min=-bound, max=bound).astype(held_as)


def setup_inputs(seed: int = 0) -> dict:
    keys = jax.random.split(jax.random.key(seed), 3)
    return {
        "populations": jnp.clip(jnp.exp(math.log(0.06) - 1.7917595 * jax.random.uniform(keys[0], (Q, NX, NY, NZ), jnp.float32) ** block_levels(keys[0], (Q, NX, NY, NZ), ((1, 32), (2, 4), (3, 4)), -0.2, 0.2)), 0.01, 0.06),
        "adjoint_next": gaussian(keys[1], (Q, NX, NY, NZ), 1.0, 6.0, ((1, 32), (2, 4), (3, 4)), jnp.float32),
    }


DIRECTIONS = ((0, 0, 0), (1, 0, 0), (-1, 0, 0), (0, 1, 0), (0, -1, 0), (0, 0, 1), (0, 0, -1), (1, 1, 0), (-1, -1, 0), (1, -1, 0), (-1, 1, 0), (1, 0, 1), (-1, 0, -1), (1, 0, -1), (-1, 0, 1), (0, 1, 1), (0, -1, -1), (0, 1, -1), (0, -1, 1))
WEIGHTS = (1.0 / 3.0,) + (1.0 / 18.0,) * 6 + (1.0 / 36.0,) * 12
RELAX_TIME = 0.8
COUPLING = -5.5

def project(vector, member):
    return DIRECTIONS[member][0] * vector[0] + DIRECTIONS[member][1] * vector[1] + DIRECTIONS[member][2] * vector[2]

def summed(populations):
    density = populations[0]
    for member in range(1, 19):
        density = density + populations[member]
    return density

def collide(populations, force_field):
    density = summed(populations)
    velocity = []
    for component in range(3):
        moment = 0.5 * force_field[component]
        for member in range(1, 19):
            heading = DIRECTIONS[member][component]
            if heading == 1:
                moment = moment + populations[member]
            elif heading == -1:
                moment = moment - populations[member]
        velocity.append(moment / density)
    speed_sq = velocity[0] * velocity[0] + velocity[1] * velocity[1] + velocity[2] * velocity[2]
    along_force = velocity[0] * force_field[0] + velocity[1] * force_field[1] + velocity[2] * force_field[2]
    results = []
    for member in range(19):
        lattice_u = project(velocity, member)
        lattice_f = project(force_field, member)
        equilibrium = WEIGHTS[member] * density * (1.0 + 3.0 * lattice_u + 4.5 * lattice_u * lattice_u - 1.5 * speed_sq)
        source = WEIGHTS[member] * (3.0 * (lattice_f - along_force) + 9.0 * lattice_u * lattice_f)
        results.append(populations[member] - (populations[member] - equilibrium) / RELAX_TIME + (1.0 - 0.5 / RELAX_TIME) * source)
    return jnp.stack(results)

def shifted(field_in, offset, direction_sign):
    return jnp.roll(field_in, (-direction_sign * offset[0], -direction_sign * offset[1], -direction_sign * offset[2]), (0, 1, 2))

def by_blocks(values_in):
    leading = values_in.shape[0]
    return values_in.reshape(leading, N_GX, NX // N_GX, NY, NZ).transpose(1, 0, 2, 3, 4)

def from_blocks(values_in):
    leading = values_in.shape[1]
    return values_in.transpose(1, 0, 2, 3, 4).reshape(leading, NX, NY, NZ)

def pulled(block_items):
    populations, force_field, arrived = block_items
    unused, pullback = jax.vjp(collide, populations, force_field)
    return pullback(arrived)

def reference(populations, adjoint_next):
    density = summed(populations)
    decay_factor = jnp.exp(-density)
    potential = 1.0 - decay_factor
    gradient = [jnp.zeros_like(potential) for component in range(3)]
    for member in range(1, 19):
        neighbour = WEIGHTS[member] * shifted(potential, DIRECTIONS[member], 1)
        for component in range(3):
            if DIRECTIONS[member][component] != 0:
                gradient[component] = gradient[component] + DIRECTIONS[member][component] * neighbour
    force_field = jnp.stack([-COUPLING * potential * gradient[component] for component in range(3)])
    arrived = jnp.stack([shifted(adjoint_next[member], DIRECTIONS[member], 1) for member in range(19)])
    pop_bar, force_bar = lax.map(pulled, (by_blocks(populations), by_blocks(force_field), by_blocks(arrived)))
    pop_bar = from_blocks(pop_bar)
    force_bar = from_blocks(force_bar)
    flux_field = potential[None] * force_bar
    remote = jnp.zeros_like(potential)
    for member in range(1, 19):
        share_part = WEIGHTS[member] * project(flux_field, member)
        remote = remote + shifted(share_part, DIRECTIONS[member], -1)
    local_part = force_bar[0] * gradient[0] + force_bar[1] * gradient[1] + force_bar[2] * gradient[2]
    potential_bar = -COUPLING * (local_part + remote)
    return pop_bar + (potential_bar * decay_factor)[None]
```

```python
import jax
import jax.numpy as jnp
from jax import lax
from jax.experimental import pallas as pl
from jax.experimental.pallas import tpu as pltpu
from jax.sharding import PartitionSpec as P

DIRECTIONS = (
    (0, 0, 0),
    (1, 0, 0),
    (-1, 0, 0),
    (0, 1, 0),
    (0, -1, 0),
    (0, 0, 1),
    (0, 0, -1),
    (1, 1, 0),
    (-1, -1, 0),
    (1, -1, 0),
    (-1, 1, 0),
    (1, 0, 1),
    (-1, 0, -1),
    (1, 0, -1),
    (-1, 0, 1),
    (0, 1, 1),
    (0, -1, -1),
    (0, 1, -1),
    (0, -1, 1),
)
W0, W1, W2 = 1.0 / 3.0, 1.0 / 18.0, 1.0 / 36.0
OMEGA = 1.0 / 0.8
KAPPA = 1.0 - 0.5 / 0.8
COUPLING = -5.5

ORDER = (1, 7, 9, 11, 13, 19, 2, 8, 10, 12, 14, 0, 3, 4, 5, 6, 15, 16, 17, 18)
SLOT = {member: place for place, member in enumerate(ORDER)}
PSI = SLOT[19]
Y_SET = ((3, 15, 17, 7, 19, 10), (4, 16, 18, 9, 19, 8))
Z_SET = ((11, 19, 14, 5, 15, 19, 18), (13, 19, 12, 6, 17, 19, 16))
EDGE_ROWS = {11: 0, 14: 1, 15: 4, 18: 5, 13: 0, 12: 1, 17: 4, 16: 5}
LO, HI = 8, 24
MESH_ID = pl.DeviceIdType.MESH


def roll(value, amount, axis):
    return pltpu.roll(value, amount % value.shape[axis], axis)


def kernel(pop_hbm, adj_hbm, part_ref, term_ref,
           pops, pg, mom, inv, dec, zcol, tmat, rows, ys, yr, zs, zr, zer, xyr,
           fp, hs, rl, xs2, xr2, ys2, yr2, es2, zr2, xyr2,
           sem_pop, sem_adj, send1, recv1, send2, recv2):
    sizes = [lax.axis_size(name) for name in ("gx", "gy", "gz")]
    here = [lax.axis_index(name) for name in ("gx", "gy", "gz")]

    def at(offset):
        return tuple(lax.rem(h + o + n, n) for h, o, n in zip(here, offset, sizes))

    barrier = pltpu.get_barrier_semaphore()
    for member in range(1, 19):
        pl.semaphore_signal(barrier, inc=1, device_id=at(DIRECTIONS[member]), device_id_type=MESH_ID)

    pop_in = [pltpu.make_async_copy(pop_hbm.at[i], pops.at[i], sem_pop.at[i]) for i in range(19)]
    adj_in = [
        pltpu.make_async_copy(adj_hbm.at[i], pg.at[SLOT[i], pl.ds(1, 8), pl.ds(LO, 16), :], sem_adj.at[i])
        for i in range(19)
    ]
    for copy in pop_in:
        copy.start()
    for copy in adj_in:
        copy.start()

    fp[...] = jnp.zeros(fp.shape, jnp.float32)
    rows[...] = jnp.zeros(rows.shape, jnp.float32)
    lane = lax.broadcasted_iota(jnp.int32, (16, 128), 1)

    for copy in pop_in:
        copy.wait()

    def density_pass(x, carry):
        f = [pops[i, x] for i in range(19)]
        rho = f[0]
        for i in range(1, 19):
            rho = rho + f[i]
        decay = jnp.exp(-rho)
        pg[PSI, x + 1, LO:HI, :] = 1.0 - decay
        dec[x] = decay
        inv[x] = 1.0 / rho
        d = {i: f[i] - f[i + 1] for i in range(1, 19, 2)}
        mom[0, x] = d[1] + (d[7] + d[9]) + (d[11] + d[13])
        mom[1, x] = d[3] + (d[7] - d[9]) + (d[15] + d[17])
        mom[2, x] = d[5] + (d[11] - d[13]) + (d[15] - d[17])
        return carry

    lax.fori_loop(0, 8, density_pass, 0)
    for copy in adj_in:
        copy.wait()

    def z_pack(x, carry):
        gathered = jnp.zeros((16, 128), jnp.float32)
        for j in range(7):
            low = pg[SLOT[Z_SET[0][j]], x + 1, LO:HI, :]
            high = pg[SLOT[Z_SET[1][j]], x + 1, LO:HI, :]
            pair = roll(jnp.where(lane < 64, low, high), 2 * j + 1, 1)
            gathered = jnp.where((lane == 2 * j) | (lane == 2 * j + 1), pair, gathered)
        tmat[pl.ds(pl.multiple_of(x * 16, 16), 16), :] = gathered
        return carry

    lax.fori_loop(0, 8, z_pack, 0)
    faces = jnp.transpose(tmat[...])
    for j in range(7):
        zs[0, j] = faces[2 * j + 1 : 2 * j + 2, :]
        zs[1, j] = faces[2 * j : 2 * j + 1, :]
    for side in range(2):
        for k in range(6):
            ys[side, k] = pg[SLOT[Y_SET[side][k]], 1:9, LO if side == 0 else HI - 1, :]

    pl.semaphore_wait(barrier, 18)

    def exchange(member, src, dst, send, recv):
        to = at(tuple(-o for o in DIRECTIONS[member]))
        return pltpu.make_async_remote_copy(
            src_ref=src, dst_ref=dst, send_sem=send.at[member - 1], recv_sem=recv.at[member - 1],
            device_id=to, device_id_type=MESH_ID,
        )

    first = []
    for member in (5, 6, 11, 12, 13, 14, 15, 16, 17, 18, 1, 2, 3, 4, 7, 8, 9, 10):
        dx, dy, dz = DIRECTIONS[member]
        if dz != 0:
            side = 0 if dz > 0 else 1
            if dx == 0 and dy == 0:
                src, dst = zs.at[side], zr.at[side]
            else:
                src = zs.at[side, pl.ds(EDGE_ROWS[member], 2)]
                dst = zer.at[member - 11]
        elif dy == 0:
            if dx > 0:
                src = pg.at[pl.ds(0, 6), 1, pl.ds(LO, 16), :]
                dst = pg.at[pl.ds(0, 6), 9, pl.ds(LO, 16), :]
            else:
                src = pg.at[pl.ds(5, 6), 8, pl.ds(LO, 16), :]
                dst = pg.at[pl.ds(5, 6), 0, pl.ds(LO, 16), :]
        elif dx == 0:
            side = 0 if dy > 0 else 1
            src, dst = ys.at[side], yr.at[side]
        else:
            side = 0 if dy > 0 else 1
            start = 3 if Y_SET[side][3] == member else 4
            src = ys.at[side, pl.ds(start, 2), 0 if dx > 0 else 7, :]
            dst = xyr.at[member - 7]
        copy = exchange(member, src, dst, send1, recv1)
        copy.start()
        first.append(copy)
    for copy in first:
        copy.wait_recv()

    for side in range(2):
        row = HI if side == 0 else LO - 1
        for k in range(6):
            pg[SLOT[Y_SET[side][k]], 1:9, row, :] = yr[side, k]
    for member in range(7, 11):
        dx, dy, _ = DIRECTIONS[member]
        plane, row = (9 if dx > 0 else 0), (HI if dy > 0 else LO - 1)
        start = 3 if Y_SET[0 if dy > 0 else 1][3] == member else 4
        own, psi_row = (0, 1) if start == 3 else (1, 0)
        pg[SLOT[member], plane, row, :] = xyr[member - 7, own]
        pg[PSI, plane, row, :] = xyr[member - 7, psi_row]

    line = lax.broadcasted_iota(jnp.int32, (1, 128), 1)
    in_y = lax.rem(line, 16)

    def shift_compact(own, edges):
        return (
            lambda: roll(jnp.where(line >= 16, own, edges[0]), -16, 1),
            lambda: roll(jnp.where(line < 112, own, edges[1]), 16, 1),
            lambda: jnp.where(in_y == 15, roll(edges[2], 15, 1), roll(own, -1, 1)),
            lambda: jnp.where(in_y == 0, roll(edges[3], -15, 1), roll(own, 1, 1)),
        )

    for side in range(2):
        names = Z_SET[side]
        face = {names[j]: zr[side, j] for j in range(7)}
        xp, xm, yp, ym = names[0], names[2], names[4], names[6]
        edge = {}
        for member, own, psi_row in ((xp, 0, 1), (xm, 1, 0), (yp, 0, 1), (ym, 1, 0)):
            edge[member] = (zer[member - 11, own], zer[member - 11, psi_row])
        psi_edges = [edge[member][1] for member in (xp, xm, yp, ym)]
        moved = [move() for move in shift_compact(face[19], psi_edges)]
        columns = [
            shift_compact(face[xp], (edge[xp][0],) * 4)[0](),
            shift_compact(face[xm], (edge[xm][0],) * 4)[1](),
            face[names[3]],
            shift_compact(face[yp], (edge[yp][0],) * 4)[2](),
            shift_compact(face[ym], (edge[ym][0],) * 4)[3](),
            moved[0] - moved[1],
            moved[2] - moved[3],
            W1 * face[19] + W2 * (moved[0] + moved[1] + moved[2] + moved[3]),
        ]
        for j in range(8):
            rows[2 * j + side : 2 * j + side + 1, :] = columns[j]
    zcol[...] = jnp.transpose(rows[...])

    upper, lower = lane == 127, lane == 0
    Z_PAIR = {11: 0, 13: 0, 14: 1, 12: 1, 5: 2, 6: 2, 15: 3, 17: 3, 18: 4, 16: 4}

    def collide_pass(x, carry):
        block = zcol[pl.ds(pl.multiple_of(x * 16, 16), 16), :]
        pairs = [roll(block, 127 - 2 * j, 1) for j in range(8)]

        def up(value, pair):
            return jnp.where(upper, pairs[pair], roll(value, -1, 1))

        def down(value, pair):
            return jnp.where(lower, pairs[pair], roll(value, 1, 1))

        def local(slot, dx, dy):
            return pg[slot, x + (1 + dx), LO + dy : HI + dy, :]

        g = []
        for member in range(19):
            dx, dy, dz = DIRECTIONS[member]
            value = local(SLOT[member], dx, dy)
            if dz == 1:
                value = up(value, Z_PAIR[member])
            elif dz == -1:
                value = down(value, Z_PAIR[member])
            g.append(value)
            hs[4 + member, x] = (1.0 - OMEGA) * value
        s = {i: g[i] + g[i + 1] for i in range(1, 19, 2)}
        d = {i: g[i] - g[i + 1] for i in range(1, 19, 2)}
        sxy, sxz, syz = s[7] + s[9], s[11] + s[13], s[15] + s[17]
        a = W0 * g[0] + W1 * (s[1] + s[3] + s[5]) + W2 * (sxy + sxz + syz)
        b = (
            3.0 * W1 * d[1] + 3.0 * W2 * ((d[7] + d[9]) + (d[11] + d[13])),
            3.0 * W1 * d[3] + 3.0 * W2 * ((d[7] - d[9]) + (d[15] + d[17])),
            3.0 * W1 * d[5] + 3.0 * W2 * ((d[11] - d[13]) + (d[15] - d[17])),
        )
        a3 = 3.0 * a
        txx = 9.0 * W1 * s[1] + 9.0 * W2 * (sxy + sxz) - a3
        tyy = 9.0 * W1 * s[3] + 9.0 * W2 * (sxy + syz) - a3
        tzz = 9.0 * W1 * s[5] + 9.0 * W2 * (sxz + syz) - a3
        txy = 9.0 * W2 * (s[7] - s[9])
        txz = 9.0 * W2 * (s[11] - s[13])
        tyz = 9.0 * W2 * (s[15] - s[17])

        psi = local(PSI, 0, 0)
        xp, xm, yp, ym = local(PSI, 1, 0), local(PSI, -1, 0), local(PSI, 0, 1), local(PSI, 0, -1)
        along_x, along_y = xp - xm, yp - ym
        along_z = W1 * psi + W2 * (xp + xm + yp + ym)
        pp, pm = local(PSI, 1, 1), local(PSI, 1, -1)
        mp, mm = local(PSI, -1, 1), local(PSI, -1, -1)
        main, cross = pp - mm, pm - mp
        grad = (
            W1 * along_x + W2 * ((main + cross) + (up(along_x, 5) + down(along_x, 5))),
            W1 * along_y + W2 * ((main - cross) + (up(along_y, 6) + down(along_y, 6))),
            up(along_z, 7) - down(along_z, 7),
        )
        strength = -COUPLING * psi
        inverse = inv[x]
        force = [strength * c for c in grad]
        u = [(mom[c, x] + 0.5 * force[c]) * inverse for c in range(3)]
        accel = [c * inverse for c in force]

        def tensor(v):
            return (
                txx * v[0] + txy * v[1] + txz * v[2],
                txy * v[0] + tyy * v[1] + tyz * v[2],
                txz * v[0] + tyz * v[1] + tzz * v[2],
            )

        tu, w = tensor(u), tensor(accel)
        v = [b[c] + tu[c] for c in range(3)]
        force_bar = [v[c] + (0.5 * KAPPA) * w[c] for c in range(3)]
        h = [OMEGA * v[c] + KAPPA * w[c] for c in range(3)]
        for c in range(3):
            fp[c, x + 2, LO:HI, :] = psi * force_bar[c]
            hs[1 + c, x] = h[c]
        e = a + 0.5 * (u[0] * (b[0] + v[0]) + u[1] * (b[1] + v[1]) + u[2] * (b[2] + v[2]))
        near = force_bar[0] * grad[0] + force_bar[1] * grad[1] + force_bar[2] * grad[2]
        hs[0, x] = (
            OMEGA * e - (u[0] * h[0] + u[1] * h[1] + u[2] * h[2]) - COUPLING * dec[x] * near
        )
        fx, fy, fz = (psi * force_bar[c] for c in range(3))
        gathered = jnp.where(
            lane < 2, roll(fz, 1, 1), jnp.where(lane < 4, roll(fx, 3, 1), roll(fy, 5, 1))
        )
        tmat[pl.ds(pl.multiple_of(x * 16, 16), 16), :] = gathered
        return carry

    lax.fori_loop(0, 8, collide_pass, 0)

    def z_shift(value, amount):
        if amount > 0:
            return jnp.where(lane[: value.shape[0]] == 127, 0.0, roll(value, -1, 1))
        return jnp.where(lane[: value.shape[0]] == 0, 0.0, roll(value, 1, 1))

    def spread(xi):
        def at_cell(c, dx, dy):
            return fp[c, xi + dx, LO + dy : HI + dy, :]

        q = at_cell(0, 1, 0) - at_cell(0, -1, 0) + at_cell(1, 0, 1) - at_cell(1, 0, -1)
        r = at_cell(2, 1, 0) + at_cell(2, -1, 0) + at_cell(2, 0, 1) + at_cell(2, 0, -1)
        r = W1 * at_cell(2, 0, 0) + W2 * r
        corner = (
            (at_cell(0, 1, 1) + at_cell(1, 1, 1))
            - (at_cell(0, -1, -1) + at_cell(1, -1, -1))
            + (at_cell(0, 1, -1) - at_cell(1, 1, -1))
            - (at_cell(0, -1, 1) - at_cell(1, -1, 1))
        )
        q2 = W2 * q
        return W1 * q + W2 * corner + z_shift(q2 + r, 1) + z_shift(q2 - r, -1)

    faces = jnp.transpose(tmat[...])
    for side in range(2):
        sign = 1.0 if side == 0 else -1.0
        pick = 1 - side
        fz, fx, fy = (sign * faces[pick : pick + 1, :], faces[2 + pick : 3 + pick, :], faces[4 + pick : 5 + pick, :])
        px = roll(W2 * (fz + fx), -16, 1)
        mx = roll(W2 * (fz - fx), 16, 1)
        py, my = W2 * (fz + fy), W2 * (fz - fy)
        own = W1 * fz
        own = own + jnp.where(line < 112, px, 0.0) + jnp.where(line >= 16, mx, 0.0)
        own = own + jnp.where(in_y != 15, roll(py, -1, 1), 0.0) + jnp.where(in_y != 0, roll(my, 1, 1), 0.0)
        es2[5 if side == 0 else 6] = own
        for member, value in (
            (Z_SET[side][0], jnp.where(line >= 112, px, 0.0)),
            (Z_SET[side][2], jnp.where(line < 16, mx, 0.0)),
            (Z_SET[side][4], jnp.where(in_y == 15, roll(py, 15, 1), 0.0)),
            (Z_SET[side][6], jnp.where(in_y == 0, roll(my, -15, 1), 0.0)),
        ):
            es2[member] = value
    for side in range(2):
        sign = 1.0 if side == 0 else -1.0
        row = LO if side == 0 else HI - 1
        fx_p, fx_m = fp[0, 3:11, row, :], fp[0, 1:9, row, :]
        fy_p, fy_m = fp[1, 3:11, row, :], fp[1, 1:9, row, :]
        fy, fz = sign * fp[1, 2:10, row, :], fp[2, 2:10, row, :]
        ys2[side] = W1 * fy + W2 * (
            (fx_p - fx_m) + sign * (fy_p + fy_m) + z_shift(fy + fz, 1) + z_shift(fy - fz, -1)
        )
    for member in range(7, 11):
        dx, dy, _ = DIRECTIONS[member]
        plane, row = (2 if dx > 0 else 9), (LO if dy > 0 else HI - 1)
        es2[member] = W2 * (dx * fp[0, plane, row : row + 1, :] + dy * fp[1, plane, row : row + 1, :])
    xs2[0] = spread(1)
    xs2[1] = spread(10)

    second = []
    for member in (5, 6, 11, 12, 13, 14, 15, 16, 17, 18, 1, 2, 3, 4, 7, 8, 9, 10):
        dx, dy, dz = DIRECTIONS[member]
        if dz != 0:
            src, dst = es2.at[member], zr2.at[member]
        elif dy == 0:
            side = 0 if dx > 0 else 1
            src, dst = xs2.at[side], xr2.at[side]
        elif dx == 0:
            side = 0 if dy > 0 else 1
            src, dst = ys2.at[side], yr2.at[side]
        else:
            src, dst = es2.at[member], xyr2.at[member - 7]
        copy = exchange(member, src, dst, send2, recv2)
        copy.start()
        second.append(copy)

    def spread_pass(x, carry):
        rl[x] = spread(x + 2)
        base = hs[0, x]
        h = [hs[1 + c, x] for c in range(3)]
        plus = [base + c for c in h]
        minus = [base - c for c in h]
        for member in range(19):
            dx, dy, dz = DIRECTIONS[member]
            total = base
            for c, o in enumerate((dx, dy, dz)):
                if o != 0:
                    total = (plus[c] if o > 0 else minus[c]) if total is base else (
                        total + h[c] if o > 0 else total - h[c]
                    )
            part_ref[member, x] = hs[4 + member, x] + total
        return carry

    lax.fori_loop(0, 8, spread_pass, 0)

    for copy in second:
        copy.wait_recv()
    rl[7] = rl[7] + xr2[0]
    rl[0] = rl[0] + xr2[1]
    rl[:, 15, :] = rl[:, 15, :] + yr2[0]
    rl[:, 0, :] = rl[:, 0, :] + yr2[1]
    for member in range(7, 11):
        dx, dy, _ = DIRECTIONS[member]
        x, y = (7 if dx > 0 else 0), (15 if dy > 0 else 0)
        rl[x, y : y + 1, :] = rl[x, y : y + 1, :] + xyr2[member - 7]
    for side in range(2):
        total = zr2[5 + side]
        for j in (0, 2, 4, 6):
            total = total + zr2[Z_SET[side][j]]
        rows[side : side + 1, :] = total
    zcol[...] = jnp.transpose(rows[...])

    def term_pass(x, carry):
        block = roll(zcol[pl.ds(pl.multiple_of(x * 16, 16), 16), :], 127, 1)
        total = rl[x] + jnp.where(upper | lower, block, 0.0)
        term_ref[x] = COUPLING * dec[x] * total
        return carry

    lax.fori_loop(0, 8, term_pass, 0)
    for copy in first:
        copy.wait_send()
    for copy in second:
        copy.wait_send()


def per_device(populations, adjoint_next):
    f32 = jnp.float32
    part, term = pl.pallas_call(
        kernel,
        out_shape=(jax.ShapeDtypeStruct((19, 8, 16, 128), f32), jax.ShapeDtypeStruct((8, 16, 128), f32)),
        in_specs=[pl.BlockSpec(memory_space=pl.ANY)] * 2,
        out_specs=[pl.BlockSpec(memory_space=pltpu.VMEM)] * 2,
        scratch_shapes=[
            pltpu.VMEM((19, 8, 16, 128), f32),
            pltpu.VMEM((20, 10, 32, 128), f32),
            pltpu.VMEM((3, 8, 16, 128), f32),
            pltpu.VMEM((8, 16, 128), f32),
            pltpu.VMEM((8, 16, 128), f32),
            pltpu.VMEM((128, 128), f32),
            pltpu.VMEM((128, 128), f32),
            pltpu.VMEM((128, 128), f32),
            pltpu.VMEM((2, 6, 8, 128), f32),
            pltpu.VMEM((2, 6, 8, 128), f32),
            pltpu.VMEM((2, 7, 1, 128), f32),
            pltpu.VMEM((2, 7, 1, 128), f32),
            pltpu.VMEM((8, 2, 1, 128), f32),
            pltpu.VMEM((4, 2, 128), f32),
            pltpu.VMEM((3, 12, 32, 128), f32),
            pltpu.VMEM((23, 8, 16, 128), f32),
            pltpu.VMEM((8, 16, 128), f32),
            pltpu.VMEM((2, 16, 128), f32),
            pltpu.VMEM((2, 16, 128), f32),
            pltpu.VMEM((2, 8, 128), f32),
            pltpu.VMEM((2, 8, 128), f32),
            pltpu.VMEM((19, 1, 128), f32),
            pltpu.VMEM((19, 1, 128), f32),
            pltpu.VMEM((4, 1, 128), f32),
            pltpu.SemaphoreType.DMA((19,)),
            pltpu.SemaphoreType.DMA((19,)),
            pltpu.SemaphoreType.DMA((18,)),
            pltpu.SemaphoreType.DMA((18,)),
            pltpu.SemaphoreType.DMA((18,)),
            pltpu.SemaphoreType.DMA((18,)),
        ],
        compiler_params=pltpu.CompilerParams(
            collective_id=0, has_side_effects=True, vmem_limit_bytes=40 * 1024 * 1024
        ),
    )(populations, adjoint_next)
    return part + term[None]


def solution(mesh):
    return jax.shard_map(
        per_device,
        mesh=mesh,
        in_specs=(P(None, "gx", "gy", "gz"), P(None, "gx", "gy", "gz")),
        out_specs=P(None, "gx", "gy", "gz"),
        check_vma=False,
    )
```

```python
import jax
import jax.numpy as jnp
from jax import lax
from jax.experimental import pallas as pl
from jax.experimental.pallas import tpu as pltpu
from jax.sharding import PartitionSpec as P

DIRECTIONS = (
    (0, 0, 0),
    (1, 0, 0),
    (-1, 0, 0),
    (0, 1, 0),
    (0, -1, 0),
    (0, 0, 1),
    (0, 0, -1),
    (1, 1, 0),
    (-1, -1, 0),
    (1, -1, 0),
    (-1, 1, 0),
    (1, 0, 1),
    (-1, 0, -1),
    (1, 0, -1),
    (-1, 0, 1),
    (0, 1, 1),
    (0, -1, -1),
    (0, 1, -1),
    (0, -1, 1),
)
W0, W1, W2 = 1.0 / 3.0, 1.0 / 18.0, 1.0 / 36.0
OMEGA = 1.0 / 0.8
KAPPA = 1.0 - 0.5 / 0.8
COUPLING = -5.5

ORDER = (1, 7, 9, 11, 13, 19, 2, 8, 10, 12, 14, 0, 3, 4, 5, 6, 15, 16, 17, 18)
SLOT = {member: place for place, member in enumerate(ORDER)}
PSI = SLOT[19]
Y_SET = ((3, 15, 17, 7, 19, 10), (4, 16, 18, 9, 19, 8))
Z_SET = ((11, 19, 14, 5, 15, 19, 18), (13, 19, 12, 6, 17, 19, 16))
EDGE_ROWS = {11: 0, 14: 1, 15: 4, 18: 5, 13: 0, 12: 1, 17: 4, 16: 5}
LO, HI = 8, 24
MESH_ID = pl.DeviceIdType.MESH


def roll(value, amount, axis):
    return pltpu.roll(value, amount % value.shape[axis], axis)


def kernel(pop_hbm, adj_hbm, part_ref, term_ref,
           pops, pg, mom, inv, dec, zcol, tmat, rows, ys, yr, zs, zr, zer, xyr,
           fp, hs, rl, xs2, xr2, ys2, yr2, es2, zr2, xyr2,
           sem_pop, sem_adj, send1, recv1, send2, recv2):
    sizes = [lax.axis_size(name) for name in ("gx", "gy", "gz")]
    here = [lax.axis_index(name) for name in ("gx", "gy", "gz")]

    def at(offset):
        return tuple(lax.rem(h + o + n, n) for h, o, n in zip(here, offset, sizes))

    barrier = pltpu.get_barrier_semaphore()
    for member in range(1, 19):
        pl.semaphore_signal(barrier, inc=1, device_id=at(DIRECTIONS[member]), device_id_type=MESH_ID)

    pop_in = [pltpu.make_async_copy(pop_hbm.at[i], pops.at[i], sem_pop.at[i]) for i in range(19)]
    adj_in = [
        pltpu.make_async_copy(adj_hbm.at[i], pg.at[SLOT[i], pl.ds(1, 8), pl.ds(LO, 16), :], sem_adj.at[i])
        for i in range(19)
    ]
    for copy in pop_in:
        copy.start()
    for copy in adj_in:
        copy.start()

    fp[...] = jnp.zeros(fp.shape, jnp.float32)
    rows[...] = jnp.zeros(rows.shape, jnp.float32)
    lane = lax.broadcasted_iota(jnp.int32, (16, 128), 1)

    for copy in pop_in:
        copy.wait()

    def density_pass(x, carry):
        f = [pops[i, x] for i in range(19)]
        rho = f[0]
        for i in range(1, 19):
            rho = rho + f[i]
        decay = jnp.exp(-rho)
        pg[PSI, x + 1, LO:HI, :] = 1.0 - decay
        dec[x] = decay
        inv[x] = 1.0 / rho
        d = {i: f[i] - f[i + 1] for i in range(1, 19, 2)}
        mom[0, x] = d[1] + (d[7] + d[9]) + (d[11] + d[13])
        mom[1, x] = d[3] + (d[7] - d[9]) + (d[15] + d[17])
        mom[2, x] = d[5] + (d[11] - d[13]) + (d[15] - d[17])
        return carry

    lax.fori_loop(0, 8, density_pass, 0)
    for copy in adj_in:
        copy.wait()

    def z_pack(x, carry):
        gathered = jnp.zeros((16, 128), jnp.float32)
        for j in range(7):
            low = pg[SLOT[Z_SET[0][j]], x + 1, LO:HI, :]
            high = pg[SLOT[Z_SET[1][j]], x + 1, LO:HI, :]
            pair = roll(jnp.where(lane < 64, low, high), 2 * j + 1, 1)
            gathered = jnp.where((lane == 2 * j) | (lane == 2 * j + 1), pair, gathered)
        tmat[pl.ds(pl.multiple_of(x * 16, 16), 16), :] = gathered
        return carry

    lax.fori_loop(0, 8, z_pack, 0)
    faces = jnp.transpose(tmat[...])
    for j in range(7):
        zs[0, j] = faces[2 * j + 1 : 2 * j + 2, :]
        zs[1, j] = faces[2 * j : 2 * j + 1, :]
    for side in range(2):
        for k in range(6):
            ys[side, k] = pg[SLOT[Y_SET[side][k]], 1:9, LO if side == 0 else HI - 1, :]

    pl.semaphore_wait(barrier, 18)

    def exchange(member, src, dst, send, recv):
        to = at(tuple(-o for o in DIRECTIONS[member]))
        return pltpu.make_async_remote_copy(
            src_ref=src, dst_ref=dst, send_sem=send.at[member - 1], recv_sem=recv.at[member - 1],
            device_id=to, device_id_type=MESH_ID,
        )

    first = []
    for member in (5, 6, 11, 12, 13, 14, 15, 16, 17, 18, 1, 2, 3, 4, 7, 8, 9, 10):
        dx, dy, dz = DIRECTIONS[member]
        if dz != 0:
            side = 0 if dz > 0 else 1
            if dx == 0 and dy == 0:
                src, dst = zs.at[side], zr.at[side]
            else:
                src = zs.at[side, pl.ds(EDGE_ROWS[member], 2)]
                dst = zer.at[member - 11]
        elif dy == 0:
            if dx > 0:
                src = pg.at[pl.ds(0, 6), 1, pl.ds(LO, 16), :]
                dst = pg.at[pl.ds(0, 6), 9, pl.ds(LO, 16), :]
            else:
                src = pg.at[pl.ds(5, 6), 8, pl.ds(LO, 16), :]
                dst = pg.at[pl.ds(5, 6), 0, pl.ds(LO, 16), :]
        elif dx == 0:
            side = 0 if dy > 0 else 1
            src, dst = ys.at[side], yr.at[side]
        else:
            side = 0 if dy > 0 else 1
            start = 3 if Y_SET[side][3] == member else 4
            src = ys.at[side, pl.ds(start, 2), 0 if dx > 0 else 7, :]
            dst = xyr.at[member - 7]
        copy = exchange(member, src, dst, send1, recv1)
        copy.start()
        first.append(copy)
    for copy in first:
        copy.wait_recv()

    for side in range(2):
        row = HI if side == 0 else LO - 1
        for k in range(6):
            pg[SLOT[Y_SET[side][k]], 1:9, row, :] = yr[side, k]
    for member in range(7, 11):
        dx, dy, _ = DIRECTIONS[member]
        plane, row = (9 if dx > 0 else 0), (HI if dy > 0 else LO - 1)
        start = 3 if Y_SET[0 if dy > 0 else 1][3] == member else 4
        own, psi_row = (0, 1) if start == 3 else (1, 0)
        pg[SLOT[member], plane, row, :] = xyr[member - 7, own]
        pg[PSI, plane, row, :] = xyr[member - 7, psi_row]

    line = lax.broadcasted_iota(jnp.int32, (1, 128), 1)
    in_y = lax.rem(line, 16)

    def shift_compact(own, edges):
        return (
            lambda: roll(jnp.where(line >= 16, own, edges[0]), -16, 1),
            lambda: roll(jnp.where(line < 112, own, edges[1]), 16, 1),
            lambda: jnp.where(in_y == 15, roll(edges[2], 15, 1), roll(own, -1, 1)),
            lambda: jnp.where(in_y == 0, roll(edges[3], -15, 1), roll(own, 1, 1)),
        )

    for side in range(2):
        names = Z_SET[side]
        face = {names[j]: zr[side, j] for j in range(7)}
        xp, xm, yp, ym = names[0], names[2], names[4], names[6]
        edge = {}
        for member, own, psi_row in ((xp, 0, 1), (xm, 1, 0), (yp, 0, 1), (ym, 1, 0)):
            edge[member] = (zer[member - 11, own], zer[member - 11, psi_row])
        psi_edges = [edge[member][1] for member in (xp, xm, yp, ym)]
        moved = [move() for move in shift_compact(face[19], psi_edges)]
        columns = [
            shift_compact(face[xp], (edge[xp][0],) * 4)[0](),
            shift_compact(face[xm], (edge[xm][0],) * 4)[1](),
            face[names[3]],
            shift_compact(face[yp], (edge[yp][0],) * 4)[2](),
            shift_compact(face[ym], (edge[ym][0],) * 4)[3](),
            moved[0] - moved[1],
            moved[2] - moved[3],
            W1 * face[19] + W2 * (moved[0] + moved[1] + moved[2] + moved[3]),
        ]
        for j in range(8):
            rows[2 * j + side : 2 * j + side + 1, :] = columns[j]
    zcol[...] = jnp.transpose(rows[...])

    upper, lower = lane == 127, lane == 0
    Z_PAIR = {11: 0, 13: 0, 14: 1, 12: 1, 5: 2, 6: 2, 15: 3, 17: 3, 18: 4, 16: 4}

    def collide_pass(x, carry):
        block = zcol[pl.ds(pl.multiple_of(x * 16, 16), 16), :]
        pairs = [roll(block, 127 - 2 * j, 1) for j in range(8)]

        def up(value, pair):
            return jnp.where(upper, pairs[pair], roll(value, -1, 1))

        def down(value, pair):
            return jnp.where(lower, pairs[pair], roll(value, 1, 1))

        def local(slot, dx, dy):
            return pg[slot, x + (1 + dx), LO + dy : HI + dy, :]

        g = []
        for member in range(19):
            dx, dy, dz = DIRECTIONS[member]
            value = local(SLOT[member], dx, dy)
            if dz == 1:
                value = up(value, Z_PAIR[member])
            elif dz == -1:
                value = down(value, Z_PAIR[member])
            g.append(value)
            hs[4 + member, x] = (1.0 - OMEGA) * value
        s = {i: g[i] + g[i + 1] for i in range(1, 19, 2)}
        d = {i: g[i] - g[i + 1] for i in range(1, 19, 2)}
        sxy, sxz, syz = s[7] + s[9], s[11] + s[13], s[15] + s[17]
        a = W0 * g[0] + W1 * (s[1] + s[3] + s[5]) + W2 * (sxy + sxz + syz)
        b = (
            3.0 * W1 * d[1] + 3.0 * W2 * ((d[7] + d[9]) + (d[11] + d[13])),
            3.0 * W1 * d[3] + 3.0 * W2 * ((d[7] - d[9]) + (d[15] + d[17])),
            3.0 * W1 * d[5] + 3.0 * W2 * ((d[11] - d[13]) + (d[15] - d[17])),
        )
        a3 = 3.0 * a
        txx = 9.0 * W1 * s[1] + 9.0 * W2 * (sxy + sxz) - a3
        tyy = 9.0 * W1 * s[3] + 9.0 * W2 * (sxy + syz) - a3
        tzz = 9.0 * W1 * s[5] + 9.0 * W2 * (sxz + syz) - a3
        txy = 9.0 * W2 * (s[7] - s[9])
        txz = 9.0 * W2 * (s[11] - s[13])
        tyz = 9.0 * W2 * (s[15] - s[17])

        psi = local(PSI, 0, 0)
        xp, xm, yp, ym = local(PSI, 1, 0), local(PSI, -1, 0), local(PSI, 0, 1), local(PSI, 0, -1)
        along_x, along_y = xp - xm, yp - ym
        along_z = W1 * psi + W2 * (xp + xm + yp + ym)
        pp, pm = local(PSI, 1, 1), local(PSI, 1, -1)
        mp, mm = local(PSI, -1, 1), local(PSI, -1, -1)
        main, cross = pp - mm, pm - mp
        grad = (
            W1 * along_x + W2 * ((main + cross) + (up(along_x, 5) + down(along_x, 5))),
            W1 * along_y + W2 * ((main - cross) + (up(along_y, 6) + down(along_y, 6))),
            up(along_z, 7) - down(along_z, 7),
        )
        strength = -COUPLING * psi
        inverse = inv[x]
        force = [strength * c for c in grad]
        u = [(mom[c, x] + 0.5 * force[c]) * inverse for c in range(3)]
        accel = [c * inverse for c in force]

        def tensor(v):
            return (
                txx * v[0] + txy * v[1] + txz * v[2],
                txy * v[0] + tyy * v[1] + tyz * v[2],
                txz * v[0] + tyz * v[1] + tzz * v[2],
            )

        tu, w = tensor(u), tensor(accel)
        v = [b[c] + tu[c] for c in range(3)]
        force_bar = [v[c] + (0.5 * KAPPA) * w[c] for c in range(3)]
        h = [OMEGA * v[c] + KAPPA * w[c] for c in range(3)]
        for c in range(3):
            fp[c, x + 2, LO:HI, :] = psi * force_bar[c]
            hs[1 + c, x] = h[c]
        e = a + 0.5 * (u[0] * (b[0] + v[0]) + u[1] * (b[1] + v[1]) + u[2] * (b[2] + v[2]))
        near = force_bar[0] * grad[0] + force_bar[1] * grad[1] + force_bar[2] * grad[2]
        hs[0, x] = (
            OMEGA * e - (u[0] * h[0] + u[1] * h[1] + u[2] * h[2]) - COUPLING * dec[x] * near
        )
        fx, fy, fz = (psi * force_bar[c] for c in range(3))
        gathered = jnp.where(
            lane < 2, roll(fz, 1, 1), jnp.where(lane < 4, roll(fx, 3, 1), roll(fy, 5, 1))
        )
        tmat[pl.ds(pl.multiple_of(x * 16, 16), 16), :] = gathered
        return carry

    lax.fori_loop(0, 8, collide_pass, 0)

    def z_shift(value, amount):
        if amount > 0:
            return jnp.where(lane[: value.shape[0]] == 127, 0.0, roll(value, -1, 1))
        return jnp.where(lane[: value.shape[0]] == 0, 0.0, roll(value, 1, 1))

    def spread(xi):
        def at_cell(c, dx, dy):
            return fp[c, xi + dx, LO + dy : HI + dy, :]

        q = at_cell(0, 1, 0) - at_cell(0, -1, 0) + at_cell(1, 0, 1) - at_cell(1, 0, -1)
        r = at_cell(2, 1, 0) + at_cell(2, -1, 0) + at_cell(2, 0, 1) + at_cell(2, 0, -1)
        r = W1 * at_cell(2, 0, 0) + W2 * r
        corner = (
            (at_cell(0, 1, 1) + at_cell(1, 1, 1))
            - (at_cell(0, -1, -1) + at_cell(1, -1, -1))
            + (at_cell(0, 1, -1) - at_cell(1, 1, -1))
            - (at_cell(0, -1, 1) - at_cell(1, -1, 1))
        )
        q2 = W2 * q
        return W1 * q + W2 * corner + z_shift(q2 + r, 1) + z_shift(q2 - r, -1)

    faces = jnp.transpose(tmat[...])
    for side in range(2):
        sign = 1.0 if side == 0 else -1.0
        pick = 1 - side
        fz, fx, fy = (sign * faces[pick : pick + 1, :], faces[2 + pick : 3 + pick, :], faces[4 + pick : 5 + pick, :])
        px = roll(W2 * (fz + fx), -16, 1)
        mx = roll(W2 * (fz - fx), 16, 1)
        py, my = W2 * (fz + fy), W2 * (fz - fy)
        own = W1 * fz
        own = own + jnp.where(line < 112, px, 0.0) + jnp.where(line >= 16, mx, 0.0)
        own = own + jnp.where(in_y != 15, roll(py, -1, 1), 0.0) + jnp.where(in_y != 0, roll(my, 1, 1), 0.0)
        es2[5 if side == 0 else 6] = own
        for member, value in (
            (Z_SET[side][0], jnp.where(line >= 112, px, 0.0)),
            (Z_SET[side][2], jnp.where(line < 16, mx, 0.0)),
            (Z_SET[side][4], jnp.where(in_y == 15, roll(py, 15, 1), 0.0)),
            (Z_SET[side][6], jnp.where(in_y == 0, roll(my, -15, 1), 0.0)),
        ):
            es2[member] = value
    for side in range(2):
        sign = 1.0 if side == 0 else -1.0
        row = LO if side == 0 else HI - 1
        fx_p, fx_m = fp[0, 3:11, row, :], fp[0, 1:9, row, :]
        fy_p, fy_m = fp[1, 3:11, row, :], fp[1, 1:9, row, :]
        fy, fz = sign * fp[1, 2:10, row, :], fp[2, 2:10, row, :]
        ys2[side] = W1 * fy + W2 * (
            (fx_p - fx_m) + sign * (fy_p + fy_m) + z_shift(fy + fz, 1) + z_shift(fy - fz, -1)
        )
    for member in range(7, 11):
        dx, dy, _ = DIRECTIONS[member]
        plane, row = (2 if dx > 0 else 9), (LO if dy > 0 else HI - 1)
        es2[member] = W2 * (dx * fp[0, plane, row : row + 1, :] + dy * fp[1, plane, row : row + 1, :])
    xs2[0] = spread(1)
    xs2[1] = spread(10)

    second = []
    for member in (5, 6, 11, 12, 13, 14, 15, 16, 17, 18, 1, 2, 3, 4, 7, 8, 9, 10):
        dx, dy, dz = DIRECTIONS[member]
        if dz != 0:
            src, dst = es2.at[member], zr2.at[member]
        elif dy == 0:
            side = 0 if dx > 0 else 1
            src, dst = xs2.at[side], xr2.at[side]
        elif dx == 0:
            side = 0 if dy > 0 else 1
            src, dst = ys2.at[side], yr2.at[side]
        else:
            src, dst = es2.at[member], xyr2.at[member - 7]
        copy = exchange(member, src, dst, send2, recv2)
        copy.start()
        second.append(copy)

    def spread_pass(x, carry):
        rl[x] = spread(x + 2)
        base = hs[0, x]
        h = [hs[1 + c, x] for c in range(3)]
        plus = [base + c for c in h]
        minus = [base - c for c in h]
        for member in range(19):
            dx, dy, dz = DIRECTIONS[member]
            total = base
            for c, o in enumerate((dx, dy, dz)):
                if o != 0:
                    total = (plus[c] if o > 0 else minus[c]) if total is base else (
                        total + h[c] if o > 0 else total - h[c]
                    )
            part_ref[member, x] = hs[4 + member, x] + total
        return carry

    lax.fori_loop(0, 8, spread_pass, 0)

    for copy in second:
        copy.wait_recv()
    rl[7] = rl[7] + xr2[0]
    rl[0] = rl[0] + xr2[1]
    rl[:, 15, :] = rl[:, 15, :] + yr2[0]
    rl[:, 0, :] = rl[:, 0, :] + yr2[1]
    for member in range(7, 11):
        dx, dy, _ = DIRECTIONS[member]
        x, y = (7 if dx > 0 else 0), (15 if dy > 0 else 0)
        rl[x, y : y + 1, :] = rl[x, y : y + 1, :] + xyr2[member - 7]
    for side in range(2):
        total = zr2[5 + side]
        for j in (0, 2, 4, 6):
            total = total + zr2[Z_SET[side][j]]
        rows[side : side + 1, :] = total
    zcol[...] = jnp.transpose(rows[...])

    def term_pass(x, carry):
        block = roll(zcol[pl.ds(pl.multiple_of(x * 16, 16), 16), :], 127, 1)
        total = rl[x] + jnp.where(upper | lower, block, 0.0)
        term_ref[x] = COUPLING * dec[x] * total
        return carry

    lax.fori_loop(0, 8, term_pass, 0)
    for copy in first:
        copy.wait_send()
    for copy in second:
        copy.wait_send()


def per_device(populations, adjoint_next):
    f32 = jnp.float32
    part, term = pl.pallas_call(
        kernel,
        out_shape=(jax.ShapeDtypeStruct((19, 8, 16, 128), f32), jax.ShapeDtypeStruct((8, 16, 128), f32)),
        in_specs=[pl.BlockSpec(memory_space=pltpu.HBM)] * 2,
        out_specs=[pl.BlockSpec(memory_space=pltpu.VMEM)] * 2,
        scratch_shapes=[
            pltpu.VMEM((19, 8, 16, 128), f32),
            pltpu.VMEM((20, 10, 32, 128), f32),
            pltpu.VMEM((3, 8, 16, 128), f32),
            pltpu.VMEM((8, 16, 128), f32),
            pltpu.VMEM((8, 16, 128), f32),
            pltpu.VMEM((128, 128), f32),
            pltpu.VMEM((128, 128), f32),
            pltpu.VMEM((128, 128), f32),
            pltpu.VMEM((2, 6, 8, 128), f32),
            pltpu.VMEM((2, 6, 8, 128), f32),
            pltpu.VMEM((2, 7, 1, 128), f32),
            pltpu.VMEM((2, 7, 1, 128), f32),
            pltpu.VMEM((8, 2, 1, 128), f32),
            pltpu.VMEM((4, 2, 128), f32),
            pltpu.VMEM((3, 12, 32, 128), f32),
            pltpu.VMEM((23, 8, 16, 128), f32),
            pltpu.VMEM((8, 16, 128), f32),
            pltpu.VMEM((2, 16, 128), f32),
            pltpu.VMEM((2, 16, 128), f32),
            pltpu.VMEM((2, 8, 128), f32),
            pltpu.VMEM((2, 8, 128), f32),
            pltpu.VMEM((19, 1, 128), f32),
            pltpu.VMEM((19, 1, 128), f32),
            pltpu.VMEM((4, 1, 128), f32),
            pltpu.SemaphoreType.DMA((19,)),
            pltpu.SemaphoreType.DMA((19,)),
            pltpu.SemaphoreType.DMA((18,)),
            pltpu.SemaphoreType.DMA((18,)),
            pltpu.SemaphoreType.DMA((18,)),
            pltpu.SemaphoreType.DMA((18,)),
        ],
        compiler_params=pltpu.CompilerParams(
            collective_id=0, has_side_effects=True, vmem_limit_bytes=40 * 1024 * 1024
        ),
    )(pltpu.with_memory_space_constraint(populations, pltpu.HBM), pltpu.with_memory_space_constraint(adjoint_next, pltpu.HBM))
    return part + term[None]


def solution(mesh):
    return jax.shard_map(
        per_device,
        mesh=mesh,
        in_specs=(P(None, "gx", "gy", "gz"), P(None, "gx", "gy", "gz")),
        out_specs=P(None, "gx", "gy", "gz"),
        check_vma=False,
    )
```

```python
import jax
import jax.numpy as jnp
from jax import lax
from jax.experimental import pallas as pl
from jax.experimental.pallas import tpu as pltpu
from jax.sharding import PartitionSpec as P

DIRECTIONS = (
    (0, 0, 0),
    (1, 0, 0),
    (-1, 0, 0),
    (0, 1, 0),
    (0, -1, 0),
    (0, 0, 1),
    (0, 0, -1),
    (1, 1, 0),
    (-1, -1, 0),
    (1, -1, 0),
    (-1, 1, 0),
    (1, 0, 1),
    (-1, 0, -1),
    (1, 0, -1),
    (-1, 0, 1),
    (0, 1, 1),
    (0, -1, -1),
    (0, 1, -1),
    (0, -1, 1),
)
W0, W1, W2 = 1.0 / 3.0, 1.0 / 18.0, 1.0 / 36.0
OMEGA = 1.0 / 0.8
KAPPA = 1.0 - 0.5 / 0.8
COUPLING = -5.5

X_PLUS = (1, 7, 9, 11, 13)
X_ZERO = (0, 3, 4, 5, 6, 15, 16, 17, 18)
X_MINUS = (2, 8, 10, 12, 14)
RHO, MOM, RHO2 = 5, 6, 18
SLOT = {}
for place, member in enumerate(X_PLUS):
    SLOT[member] = place
for place, member in enumerate(X_ZERO):
    SLOT[member] = 9 + place
for place, member in enumerate(X_MINUS):
    SLOT[member] = 19 + place
PSI = -1
Y_SET = ((3, 15, 17, 7, PSI, 10), (4, 16, 18, 9, PSI, 8))
UP = (5, 11, 14, 15, 18)
DOWN = (6, 13, 12, 17, 16)
FLAT = (0, 1, 2, 3, 4, 7, 8, 9, 10)
QUAD = (0, 1, 4, 5, 8, 9)
LO, HI = 8, 24
MESH_ID = pl.DeviceIdType.MESH
NEAR = (
    (0, 0, 1), (0, 0, -1), (1, 0, 1), (1, 0, -1), (-1, 0, 1), (-1, 0, -1),
    (1, 1, 0), (1, -1, 0), (-1, 1, 0), (-1, -1, 0), (0, 1, 0), (0, -1, 0), (1, 0, 0), (-1, 0, 0),
)


def roll(value, amount, axis=1):
    if isinstance(amount, int):
        amount = amount % value.shape[axis]
        if amount == 0:
            return value
    return pltpu.roll(value, amount, axis)


def collide(g, rho, mom, psi, grad):
    s = {i: g[i] + g[i + 1] for i in range(1, 19, 2)}
    d = {i: g[i] - g[i + 1] for i in range(1, 19, 2)}
    sxy, sxz, syz = s[7] + s[9], s[11] + s[13], s[15] + s[17]
    a = W0 * g[0] + W1 * (s[1] + s[3] + s[5]) + W2 * (sxy + sxz + syz)
    b = (
        3.0 * W1 * d[1] + 3.0 * W2 * ((d[7] + d[9]) + (d[11] + d[13])),
        3.0 * W1 * d[3] + 3.0 * W2 * ((d[7] - d[9]) + (d[15] + d[17])),
        3.0 * W1 * d[5] + 3.0 * W2 * ((d[11] - d[13]) + (d[15] - d[17])),
    )
    a3 = 3.0 * a
    txx = 9.0 * W1 * s[1] + 9.0 * W2 * (sxy + sxz) - a3
    tyy = 9.0 * W1 * s[3] + 9.0 * W2 * (sxy + syz) - a3
    tzz = 9.0 * W1 * s[5] + 9.0 * W2 * (sxz + syz) - a3
    txy = 9.0 * W2 * (s[7] - s[9])
    txz = 9.0 * W2 * (s[11] - s[13])
    tyz = 9.0 * W2 * (s[15] - s[17])
    inverse = 1.0 / rho
    strength = -COUPLING * psi
    force = [strength * c for c in grad]
    u = [(mom[c] + 0.5 * force[c]) * inverse for c in range(3)]
    accel = [c * inverse for c in force]

    def tensor(v):
        return (
            txx * v[0] + txy * v[1] + txz * v[2],
            txy * v[0] + tyy * v[1] + tyz * v[2],
            txz * v[0] + tyz * v[1] + tzz * v[2],
        )

    tu, w = tensor(u), tensor(accel)
    v = [b[c] + tu[c] for c in range(3)]
    force_bar = [v[c] + (0.5 * KAPPA) * w[c] for c in range(3)]
    h = [OMEGA * v[c] + KAPPA * w[c] for c in range(3)]
    e = a + 0.5 * (u[0] * (b[0] + v[0]) + u[1] * (b[1] + v[1]) + u[2] * (b[2] + v[2]))
    near = force_bar[0] * grad[0] + force_bar[1] * grad[1] + force_bar[2] * grad[2]
    base = OMEGA * e - (u[0] * h[0] + u[1] * h[1] + u[2] * h[2])
    return force_bar, h, base, near


def gradient(get, up, down):
    psi = get(0, 0)
    xp, xm, yp, ym = get(1, 0), get(-1, 0), get(0, 1), get(0, -1)
    along_x, along_y = xp - xm, yp - ym
    along_z = W1 * psi + W2 * (xp + xm + yp + ym)
    main, cross = get(1, 1) - get(-1, -1), get(1, -1) - get(-1, 1)
    grad = (
        W1 * along_x + W2 * ((main + cross) + (up(along_x, 0) + down(along_x, 0))),
        W1 * along_y + W2 * ((main - cross) + (up(along_y, 1) + down(along_y, 1))),
        up(along_z, 2) - down(along_z, 2),
    )
    return psi, grad, (along_x, along_y, along_z)


def kernel(pop_hbm, adj_hbm, part_ref, term_ref,
           pops, pg, ps, density, dec, zt, zz, strip, sps, sc, fs, rs, fp, hs, rl,
           ys, yr, ye, bs, br, cs, cr,
           sem_pop, sem_adj, send, recv, send_y, recv_y):
    sizes = [lax.axis_size(name) for name in ("gx", "gy", "gz")]
    here = [lax.axis_index(name) for name in ("gx", "gy", "gz")]

    def at(offset):
        return tuple(lax.rem(h + o + n, n) for h, o, n in zip(here, offset, sizes))

    barrier = pltpu.get_barrier_semaphore()
    for offset in NEAR:
        pl.semaphore_signal(barrier, inc=1, device_id=at(offset), device_id_type=MESH_ID)
    own = pl.ds(2, 8)
    pop_in = [pltpu.make_async_copy(pop_hbm.at[i], pops.at[i], sem_pop.at[i]) for i in range(19)]
    adj_in = [
        pltpu.make_async_copy(adj_hbm.at[i], pg.at[SLOT[i], own, pl.ds(LO, 16), :], sem_adj.at[i]) for i in range(19)
    ]
    for copy in pop_in + adj_in:
        copy.start()
    lane = lax.broadcasted_iota(jnp.int32, (16, 128), 1)
    lane8 = lane[:8]
    upper, lower = lane == 127, lane == 0
    for ref in (sps, fs, strip, fp):
        ref[...] = jnp.zeros(ref.shape, jnp.float32)
    for copy in pop_in:
        copy.wait()

    def density_pass(x, carry):
        f = [pops[i, x] for i in range(19)]
        rho = f[0]
        for i in range(1, 19):
            rho = rho + f[i]
        decay = jnp.exp(-rho)
        pg[RHO, x + 2, LO:HI, :] = rho
        pg[RHO2, x + 2, LO:HI, :] = rho
        density[x + 2] = rho
        dec[x] = decay
        ps[x + 2, LO:HI, :] = 1.0 - decay
        d = {i: f[i] - f[i + 1] for i in range(1, 19, 2)}
        pg[MOM, x + 2, LO:HI, :] = d[1] + (d[7] + d[9]) + (d[11] + d[13])
        pg[MOM + 1, x + 2, LO:HI, :] = d[3] + (d[7] - d[9]) + (d[15] + d[17])
        pg[MOM + 2, x + 2, LO:HI, :] = d[5] + (d[11] - d[13]) + (d[15] - d[17])
        return carry

    lax.fori_loop(0, 8, density_pass, 0)
    for copy in adj_in:
        copy.wait()

    def pack(x, carry):
        up_a, up_b, low_q, low_a, low_b = carry

        def split(j):
            if j == 5:
                return pg[RHO, x + 2, LO:HI, :]
            return jnp.where(lane < 64, pg[SLOT[UP[j]], x + 2, LO:HI, :], pg[SLOT[DOWN[j]], x + 2, LO:HI, :])

        for j in range(6):
            value = split(j)
            for deeper in range(2):
                target = 8 * (QUAD[j] + 2 * deeper) + x
                moved = roll(value, lax.rem(target + 128 - deeper, 128))
                up_a = jnp.where(lane == target, moved, up_a)
                low_q = jnp.where(lane == lax.rem(target + 126, 128), moved, low_q)
        for j in range(12):
            value = pg[SLOT[FLAT[j]], x + 2, LO:HI, :] if j < 9 else pg[MOM + j - 9, x + 2, LO:HI, :]
            target = 8 * ((12 + j) % 16) + x
            moved = roll(value, target)
            mark, low_mark = lane == target, lane == lax.rem(target + 127, 128)
            if j < 4:
                up_a = jnp.where(mark, moved, up_a)
                low_a = jnp.where(low_mark, moved, low_a)
            else:
                up_b = jnp.where(mark, moved, up_b)
                low_b = jnp.where(low_mark, moved, low_b)
        return up_a, up_b, low_q, low_a, low_b

    nothing = jnp.zeros((16, 128), jnp.float32)
    up_a, up_b, low_q, low_a, low_b = lax.fori_loop(0, 8, pack, (nothing,) * 5)
    low_a = jnp.where(lane < 96, roll(low_q, 2), roll(low_a, 1))
    low_b = roll(low_b, 1)
    in_eight = lax.rem(lane, 8)
    for side, (a, b) in enumerate(((up_a, up_b), (low_a, low_b))):
        zt[2 * side] = a
        zt[2 * side + 1] = b
        zt[4 + side] = jnp.where(
            (in_eight < 2) | (in_eight >= 6), a, jnp.where(in_eight < 4, roll(b, 2), roll(b, -2))
        )

    for side in range(2):
        row = LO if side == 0 else HI - 1
        for k in range(6):
            member = Y_SET[side][k]
            ys[side, k] = ps[2:10, row, :] if member == PSI else pg[SLOT[member], 2:10, row, :]
    pl.semaphore_wait(barrier, len(NEAR))

    def copy_to(offset, src, dst, sends, recvs, index):
        return pltpu.make_async_remote_copy(
            src_ref=src, dst_ref=dst, send_sem=sends.at[index], recv_sem=recvs.at[index],
            device_id=at(tuple(-o for o in offset)), device_id_type=MESH_ID,
        )

    def message(index, offset, src, dst):
        return copy_to(offset, src, dst, send, recv, index)

    z_copies, y_copies, x_copies = [], [], []
    block = pl.ds(LO, 16)
    for offset in NEAR:
        dx, dy, dz = offset
        if dz != 0:
            side = 0 if dz > 0 else 1
            if dx == 0:
                z_copies.append(message(side, offset, zt.at[pl.ds(2 * side, 2)], zz.at[pl.ds(2 * side, 2)]))
            else:
                xs = 0 if dx > 0 else 1
                z_copies.append(
                    message(2 + 2 * side + xs, offset, zt.at[4 + side], zz.at[4 + 2 * side + xs])
                )
    for xs in range(2):
        offset = (1 - 2 * xs, 0, 0)
        z_copies.append(message(6 + xs, offset, zt.at[pl.ds(4, 2)], zz.at[pl.ds(8 + 2 * xs, 2)]))
    for side in range(2):
        for xs in range(2):
            offset = (1 - 2 * xs, 1 - 2 * side, 0)
            src = ys.at[side, :, pl.ds(0 if xs == 0 else 6, 2), :]
            y_copies.append(message(8 + 2 * side + xs, offset, src, ye.at[2 * side + xs]))
        y_copies.append(message(12 + side, (0, 1 - 2 * side, 0), ys.at[side], yr.at[side]))
    for xs in range(2):
        offset = (1 - 2 * xs, 0, 0)
        if xs == 0:
            parts = ((pl.ds(0, 18), 2, 10), (pl.ds(0, 6), 3, 11))
        else:
            parts = ((pl.ds(6, 18), 9, 1), (pl.ds(18, 6), 8, 0))
        for k, (slots, near, far) in enumerate(parts):
            x_copies.append(
                message(14 + 2 * xs + k, offset, pg.at[slots, near, block, :], pg.at[slots, far, block, :])
            )
    for copy in z_copies + y_copies + x_copies:
        copy.start()

    for copy in y_copies:
        copy.wait_recv()
    for side in range(2):
        row = HI if side == 0 else LO - 1
        for k in range(6):
            member = Y_SET[side][k]
            for start, count, value in ((2, 8, yr[side, k]), (10, 2, ye[2 * side, k]), (0, 2, ye[2 * side + 1, k])):
                if member == PSI:
                    ps[start : start + count, row, :] = value
                else:
                    pg[SLOT[member], start : start + count, row, :] = value
    for copy in z_copies:
        copy.wait_recv()

    def span(start, count):
        return (lane >= start) & (lane < start + count)

    def fill(value, side, spot, group, deep, cx, own):
        tiles = (zt.at[2 * side], zt.at[2 * side + 1]) if own else (zz.at[2 * side], zz.at[2 * side + 1])
        local = spot % 16
        mark = span(16 * group + 2, 8)
        if deep:
            mark = mark | span(16 * group + 18, 8)
        value = jnp.where(mark, roll(tiles[spot // 16][...], 16 * group + 2 - 8 * local), value)
        for xs, start, low, high in ((0, 10, 0, 2), (1, 0, 6, 4)):
            if cx is not None and cx == (-1 if xs == 0 else 1):
                continue
            tile = zz[8 + 2 * xs + side] if own else zz[4 + 2 * side + xs]
            source = 8 * local + (low if spot < 16 else high)
            mark = span(16 * group + start, 2)
            if deep:
                mark = mark | span(16 * group + 16 + start, 2)
            value = jnp.where(mark, roll(tile, 16 * group + start - source), value)
        return value

    for j in range(5):
        cx = DIRECTIONS[UP[j]][0]
        value = fill(nothing, 0, QUAD[j], 4, True, cx, False)
        strip[SLOT[UP[j]], LO:HI, :] = fill(value, 0, QUAD[j], 2, False, cx, True)
        cx = DIRECTIONS[DOWN[j]][0]
        value = fill(nothing, 1, QUAD[j], 0, True, cx, False)
        strip[SLOT[DOWN[j]], LO:HI, :] = fill(value, 1, QUAD[j] + 2, 3, False, cx, True)
    for j in range(12):
        slot, cx = (SLOT[FLAT[j]], DIRECTIONS[FLAT[j]][0]) if j < 9 else (MOM + j - 9, None)
        value = fill(nothing, 0, 12 + j, 4, False, cx, False)
        strip[slot, LO:HI, :] = fill(value, 1, 12 + j, 1, False, cx, False)
    value = fill(nothing, 0, QUAD[5], 4, True, None, False)
    value = fill(value, 0, QUAD[5], 2, False, None, True)
    value = fill(value, 1, QUAD[5], 0, True, None, False)
    value = fill(value, 1, QUAD[5] + 2, 3, False, None, True)
    strip[RHO, LO:HI, :] = value
    sps[LO:HI, :] = 1.0 - jnp.exp(-value)

    def strip_row(member):
        return sps if member == PSI else strip.at[SLOT[member]]

    def along_y(side, src, dst, index):
        return copy_to((0, 1 - 2 * side, 0), src, dst, send_y, recv_y, index)

    for side in range(2):
        row = LO if side == 0 else HI - 1
        for k in range(6):
            bs[side, k : k + 1, :] = strip_row(Y_SET[side][k])[row : row + 1, :]
    y_first = [along_y(side, bs.at[side], br.at[side], side) for side in range(2)]
    for copy in y_first:
        copy.start()
    for copy in y_first:
        copy.wait_recv()
    for side in range(2):
        row = HI if side == 0 else LO - 1
        for k in range(6):
            strip_row(Y_SET[side][k])[row : row + 1, :] = br[side, k : k + 1, :]

    g = []
    for member in range(19):
        dx, dy, dz = DIRECTIONS[member]
        g.append(roll(strip[SLOT[member], LO + dy : HI + dy, :], -(16 * dz + dx)))
    psi, grad, along = gradient(
        lambda dx, dy: roll(sps[LO + dy : HI + dy, :], -dx),
        lambda value, _: roll(value, -16),
        lambda value, _: roll(value, 16),
    )
    for c in range(3):
        sc[c] = along[c]
    above, below = span(64, 16), span(16, 16)
    inside = span(65, 10) | span(17, 10)
    own_rho = jnp.where(inside, strip[RHO, LO:HI, :], 1.0)
    force_bar, _, _, _ = collide(g, own_rho, [strip[MOM + c, LO:HI, :] for c in range(3)], psi, grad)
    for c in range(3):
        fs[c, LO:HI, :] = jnp.where(inside, psi * force_bar[c], 0.0)

    def signed(value):
        return jnp.where(above[: value.shape[0]], value, -value)

    fx, fz = fs[0, LO:HI, :], signed(fs[2, LO:HI, :])
    spill = W1 * fz + W2 * (
        roll(fx + fz, -1) - roll(fx - fz, 1)
        + (fs[1, LO + 1 : HI + 1, :] + signed(fs[2, LO + 1 : HI + 1, :]))
        - (fs[1, LO - 1 : HI - 1, :] - signed(fs[2, LO - 1 : HI - 1, :]))
    )
    rs[...] = spill

    def collide_pass(xi, carry):
        def up(value, inner):
            return jnp.where(upper, inner, roll(value, -1))

        def down(value, inner):
            return jnp.where(lower, inner, roll(value, 1))

        g = []
        for member in range(19):
            dx, dy, dz = DIRECTIONS[member]
            value = pg[SLOT[member], xi + dx, LO + dy : HI + dy, :]
            if dz != 0:
                edge = strip[SLOT[member], LO + dy : HI + dy, :]
                if dz > 0:
                    value = up(value, roll(edge, 63 - dx - xi))
                else:
                    value = down(value, roll(edge, 112 - dx - xi))
            g.append(value)
            hs[4 + member, xi] = (1.0 - OMEGA) * value
        psi, grad, _ = gradient(
            lambda dx, dy: ps[xi + dx, LO + dy : HI + dy, :],
            lambda value, key: up(value, roll(sc[key], 63 - xi)),
            lambda value, key: down(value, roll(sc[key], 112 - xi)),
        )
        force_bar, h, base, near = collide(
            g, density[xi], [pg[MOM + c, xi, LO:HI, :] for c in range(3)], psi, grad
        )
        for c in range(3):
            fp[c, xi, LO:HI, :] = psi * force_bar[c]
            hs[1 + c, xi] = h[c]
        hs[0, xi] = base - COUPLING * ((1.0 - psi) * near)
        return carry

    lax.fori_loop(3, 9, collide_pass, 0)
    for copy in x_copies:
        copy.wait_recv()
    for xi, slot in ((0, RHO2), (1, RHO2), (10, RHO), (11, RHO)):
        value = pg[slot, xi, LO:HI, :]
        density[xi] = value
        ps[xi, LO:HI, :] = 1.0 - jnp.exp(-value)
    lax.fori_loop(1, 3, collide_pass, 0)
    lax.fori_loop(9, 11, collide_pass, 0)

    sub8 = lax.broadcasted_iota(jnp.int32, (8, 128), 0)
    for side in range(2):
        sign = 1.0 if side == 0 else -1.0
        row = LO if side == 0 else HI - 1

        def column(value, start):
            picked = jnp.where(lane8 == sub8 + start, jnp.broadcast_to(value, (8, 128)), 0.0)
            return jnp.sum(picked, axis=1, keepdims=True)

        fx_p, fx_m = fp[0, 3:11, row, :], fp[0, 1:9, row, :]
        fy_p, fy_m = fp[1, 3:11, row, :], fp[1, 1:9, row, :]
        fy, fz = sign * fp[1, 2:10, row, :], fp[2, 2:10, row, :]
        sy, sz = sign * fs[1, row : row + 1, :], fs[2, row : row + 1, :]
        over = jnp.where(lane8 == 127, column(sy + sz, 66), roll(fy + fz, -1))
        under = jnp.where(lane8 == 0, column(sy - sz, 18), roll(fy - fz, 1))
        cs[side] = W1 * fy + W2 * ((fx_p - fx_m) + sign * (fy_p + fy_m) + over + under)
    y_second = [along_y(side, cs.at[side], cr.at[side], 2 + side) for side in range(2)]
    for copy in y_second:
        copy.start()

    def spread_pass(x, carry):
        xi = x + 2

        def cell(c, dx, dy):
            return fp[c, xi + dx, LO + dy : HI + dy, :]

        q = cell(0, 1, 0) - cell(0, -1, 0) + cell(1, 0, 1) - cell(1, 0, -1)
        r = cell(2, 1, 0) + cell(2, -1, 0) + cell(2, 0, 1) + cell(2, 0, -1)
        r = W1 * cell(2, 0, 0) + W2 * r
        corner = (
            (cell(0, 1, 1) + cell(1, 1, 1))
            - (cell(0, -1, -1) + cell(1, -1, -1))
            + (cell(0, 1, -1) - cell(1, 1, -1))
            - (cell(0, -1, 1) - cell(1, -1, 1))
        )
        q2 = W2 * q
        outer = rs[...]
        over = jnp.where(upper, roll(outer, 63 - xi), roll(q2 + r, -1))
        under = jnp.where(lower, roll(outer, 112 - xi), roll(q2 - r, 1))
        rl[x] = W1 * q + W2 * corner + over + under
        base = hs[0, xi]
        h = [hs[1 + c, xi] for c in range(3)]
        plus = [base + c for c in h]
        minus = [base - c for c in h]
        for member in range(19):
            total = base
            for c, o in enumerate(DIRECTIONS[member]):
                if o != 0:
                    total = (plus[c] if o > 0 else minus[c]) if total is base else (
                        total + h[c] if o > 0 else total - h[c]
                    )
            part_ref[member, x] = hs[4 + member, xi] + total
        return carry

    lax.fori_loop(0, 8, spread_pass, 0)

    for copy in y_second:
        copy.wait_recv()
    rl[:, 15, :] = rl[:, 15, :] + cr[0]
    rl[:, 0, :] = rl[:, 0, :] + cr[1]
    term_ref[...] = COUPLING * dec[...] * rl[...]
    for copy in z_copies + y_copies + x_copies + y_first + y_second:
        copy.wait_send()


def per_device(populations, adjoint_next):
    f32 = jnp.float32
    dma = pltpu.SemaphoreType.DMA
    shapes = (
        (19, 8, 16, 128),
        (24, 12, 32, 128),
        (12, 32, 128),
        (12, 16, 128),
        (8, 16, 128),
        (6, 16, 128),
        (12, 16, 128),
        (24, 32, 128),
        (32, 128),
        (3, 16, 128),
        (3, 32, 128),
        (16, 128),
        (3, 12, 32, 128),
        (23, 12, 16, 128),
        (8, 16, 128),
        (2, 6, 8, 128),
        (2, 6, 8, 128),
        (4, 6, 2, 128),
        (2, 8, 128),
        (2, 8, 128),
        (2, 8, 128),
        (2, 8, 128),
    )
    part, term = pl.pallas_call(
        kernel,
        out_shape=[jax.ShapeDtypeStruct((19, 8, 16, 128), f32), jax.ShapeDtypeStruct((8, 16, 128), f32)],
        in_specs=[pl.BlockSpec(memory_space=pl.ANY)] * 2,
        out_specs=[pl.BlockSpec(memory_space=pltpu.VMEM)] * 2,
        scratch_shapes=[pltpu.VMEM(shape, f32) for shape in shapes]
        + [dma((19,)), dma((19,)), dma((18,)), dma((18,)), dma((4,)), dma((4,))],
        compiler_params=pltpu.CompilerParams(
            collective_id=0, has_side_effects=True, vmem_limit_bytes=40 * 1024 * 1024
        ),
    )(
        pltpu.with_memory_space_constraint(populations, pltpu.HBM),
        pltpu.with_memory_space_constraint(adjoint_next, pltpu.HBM),
    )
    return part + term[None]


def solution(mesh):
    return jax.shard_map(
        per_device,
        mesh=mesh,
        in_specs=(P(None, "gx", "gy", "gz"), P(None, "gx", "gy", "gz")),
        out_specs=P(None, "gx", "gy", "gz"),
        check_vma=False,
    )
```

```python
import jax
import jax.numpy as jnp
from jax import lax
from jax.experimental import pallas as pl
from jax.experimental.pallas import tpu as pltpu
from jax.sharding import PartitionSpec as P

DIRECTIONS = (
    (0, 0, 0),
    (1, 0, 0),
    (-1, 0, 0),
    (0, 1, 0),
    (0, -1, 0),
    (0, 0, 1),
    (0, 0, -1),
    (1, 1, 0),
    (-1, -1, 0),
    (1, -1, 0),
    (-1, 1, 0),
    (1, 0, 1),
    (-1, 0, -1),
    (1, 0, -1),
    (-1, 0, 1),
    (0, 1, 1),
    (0, -1, -1),
    (0, 1, -1),
    (0, -1, 1),
)
W0, W1, W2 = 1.0 / 3.0, 1.0 / 18.0, 1.0 / 36.0
OMEGA = 1.0 / 0.8
KAPPA = 1.0 - 0.5 / 0.8
COUPLING = -5.5

X_PLUS = (1, 7, 9, 11, 13)
X_ZERO = (0, 3, 4, 5, 6, 15, 16, 17, 18)
X_MINUS = (2, 8, 10, 12, 14)
RHO, MOM, RHO2 = 5, 6, 18
SLOT = {}
for place, member in enumerate(X_PLUS):
    SLOT[member] = place
for place, member in enumerate(X_ZERO):
    SLOT[member] = 9 + place
for place, member in enumerate(X_MINUS):
    SLOT[member] = 19 + place
PSI = -1
Y_SET = ((3, 15, 17, 7, PSI, 10), (4, 16, 18, 9, PSI, 8))
UP = (5, 11, 14, 15, 18)
DOWN = (6, 13, 12, 17, 16)
FLAT = (0, 1, 2, 3, 4, 7, 8, 9, 10)
QUAD = (0, 1, 4, 5, 8, 9)
LO, HI = 8, 24
MESH_ID = pl.DeviceIdType.MESH
NEAR = (
    (0, 0, 1), (0, 0, -1), (1, 0, 1), (1, 0, -1), (-1, 0, 1), (-1, 0, -1),
    (1, 1, 0), (1, -1, 0), (-1, 1, 0), (-1, -1, 0), (0, 1, 0), (0, -1, 0), (1, 0, 0), (-1, 0, 0),
)


def roll(value, amount, axis=1):
    if isinstance(amount, int):
        amount = amount % value.shape[axis]
        if amount == 0:
            return value
    return pltpu.roll(value, amount, axis)


def collide(g, rho, mom, psi, grad):
    s = {i: g[i] + g[i + 1] for i in range(1, 19, 2)}
    d = {i: g[i] - g[i + 1] for i in range(1, 19, 2)}
    sxy, sxz, syz = s[7] + s[9], s[11] + s[13], s[15] + s[17]
    a = W0 * g[0] + W1 * (s[1] + s[3] + s[5]) + W2 * (sxy + sxz + syz)
    b = (
        3.0 * W1 * d[1] + 3.0 * W2 * ((d[7] + d[9]) + (d[11] + d[13])),
        3.0 * W1 * d[3] + 3.0 * W2 * ((d[7] - d[9]) + (d[15] + d[17])),
        3.0 * W1 * d[5] + 3.0 * W2 * ((d[11] - d[13]) + (d[15] - d[17])),
    )
    a3 = 3.0 * a
    txx = 9.0 * W1 * s[1] + 9.0 * W2 * (sxy + sxz) - a3
    tyy = 9.0 * W1 * s[3] + 9.0 * W2 * (sxy + syz) - a3
    tzz = 9.0 * W1 * s[5] + 9.0 * W2 * (sxz + syz) - a3
    txy = 9.0 * W2 * (s[7] - s[9])
    txz = 9.0 * W2 * (s[11] - s[13])
    tyz = 9.0 * W2 * (s[15] - s[17])
    inverse = 1.0 / rho
    strength = -COUPLING * psi
    force = [strength * c for c in grad]
    u = [(mom[c] + 0.5 * force[c]) * inverse for c in range(3)]
    accel = [c * inverse for c in force]

    def tensor(v):
        return (
            txx * v[0] + txy * v[1] + txz * v[2],
            txy * v[0] + tyy * v[1] + tyz * v[2],
            txz * v[0] + tyz * v[1] + tzz * v[2],
        )

    tu, w = tensor(u), tensor(accel)
    v = [b[c] + tu[c] for c in range(3)]
    force_bar = [v[c] + (0.5 * KAPPA) * w[c] for c in range(3)]
    h = [OMEGA * v[c] + KAPPA * w[c] for c in range(3)]
    e = a + 0.5 * (u[0] * (b[0] + v[0]) + u[1] * (b[1] + v[1]) + u[2] * (b[2] + v[2]))
    near = force_bar[0] * grad[0] + force_bar[1] * grad[1] + force_bar[2] * grad[2]
    base = OMEGA * e - (u[0] * h[0] + u[1] * h[1] + u[2] * h[2])
    return force_bar, h, base, near


def gradient(get, up, down):
    psi = get(0, 0)
    xp, xm, yp, ym = get(1, 0), get(-1, 0), get(0, 1), get(0, -1)
    along_x, along_y = xp - xm, yp - ym
    along_z = W1 * psi + W2 * (xp + xm + yp + ym)
    main, cross = get(1, 1) - get(-1, -1), get(1, -1) - get(-1, 1)
    grad = (
        W1 * along_x + W2 * ((main + cross) + (up(along_x) + down(along_x))),
        W1 * along_y + W2 * ((main - cross) + (up(along_y) + down(along_y))),
        up(along_z) - down(along_z),
    )
    return psi, grad


def kernel(pop_hbm, adj_hbm, part_ref, term_ref,
           pops, pg, ps, density, dec, zt, zz, strip, sps, so, fs, rs, fp, hs, rl,
           ys, yr, ye, yx, bs, br, cs, cr,
           ready, sem_pop, sem_adj, send, recv, send_y, recv_y):
    sizes = [lax.axis_size(name) for name in ("gx", "gy", "gz")]
    here = [lax.axis_index(name) for name in ("gx", "gy", "gz")]

    def at(offset):
        return tuple(lax.rem(h + o + n, n) for h, o, n in zip(here, offset, sizes))

    def ages(offset):
        (px, _, pz), (x, _, z) = at(offset), here
        half = sizes[2] // 2
        low, other_low = (z < half).astype(jnp.int32), (pz < half).astype(jnp.int32)
        wrap = (jnp.abs(px - x) > 1).astype(jnp.int32) * (low == other_low).astype(jnp.int32)
        other = other_low * (1 - low) + wrap * (px == 0).astype(jnp.int32)
        own = low * (1 - other_low) + wrap * (x == 0).astype(jnp.int32)
        return other, own

    def opposite(offset):
        return tuple(-o for o in offset)

    barrier = pltpu.get_barrier_semaphore()
    expected = 0
    for offset in NEAR:
        other_elder, own_elder = ages(offset)
        expected = expected + (1 - own_elder)

        @pl.when(other_elder == 0)
        def _():
            pl.semaphore_signal(barrier, inc=1, device_id=at(offset), device_id_type=MESH_ID)

    own = pl.ds(2, 8)
    pop_in = [pltpu.make_async_copy(pop_hbm.at[i], pops.at[i], sem_pop.at[i]) for i in range(19)]
    adj_in = [
        pltpu.make_async_copy(adj_hbm.at[i], pg.at[SLOT[i], own, pl.ds(LO, 16), :], sem_adj.at[i]) for i in range(19)
    ]
    for copy in pop_in + adj_in:
        copy.start()
    lane = lax.broadcasted_iota(jnp.int32, (16, 128), 1)
    lane8 = lane[:8]
    upper, lower = lane == 127, lane == 0
    for ref in (sps, fs, strip, fp):
        ref[...] = jnp.zeros(ref.shape, jnp.float32)
    for copy in pop_in:
        copy.wait()

    def density_pass(x, carry):
        f = [pops[i, x] for i in range(19)]
        rho = f[0]
        for i in range(1, 19):
            rho = rho + f[i]
        decay = jnp.exp(-rho)
        pg[RHO, x + 2, LO:HI, :] = rho
        pg[RHO2, x + 2, LO:HI, :] = rho
        density[x + 2] = rho
        dec[x] = decay
        ps[x + 2, LO:HI, :] = 1.0 - decay
        d = {i: f[i] - f[i + 1] for i in range(1, 19, 2)}
        pg[MOM, x + 2, LO:HI, :] = d[1] + (d[7] + d[9]) + (d[11] + d[13])
        pg[MOM + 1, x + 2, LO:HI, :] = d[3] + (d[7] - d[9]) + (d[15] + d[17])
        pg[MOM + 2, x + 2, LO:HI, :] = d[5] + (d[11] - d[13]) + (d[15] - d[17])
        return carry

    lax.fori_loop(0, 8, density_pass, 0)
    for copy in adj_in:
        copy.wait()

    def pack(x, carry):
        up_a, up_b, low_q, low_a, low_b = carry

        def split(j):
            if j == 5:
                return pg[RHO, x + 2, LO:HI, :]
            return jnp.where(lane < 64, pg[SLOT[UP[j]], x + 2, LO:HI, :], pg[SLOT[DOWN[j]], x + 2, LO:HI, :])

        for j in range(6):
            value = split(j)
            for deeper in range(2):
                target = 8 * (QUAD[j] + 2 * deeper) + x
                moved = roll(value, lax.rem(target + 128 - deeper, 128))
                up_a = jnp.where(lane == target, moved, up_a)
                low_q = jnp.where(lane == lax.rem(target + 126, 128), moved, low_q)
        for j in range(12):
            value = pg[SLOT[FLAT[j]], x + 2, LO:HI, :] if j < 9 else pg[MOM + j - 9, x + 2, LO:HI, :]
            target = 8 * ((12 + j) % 16) + x
            moved = roll(value, target)
            mark, low_mark = lane == target, lane == lax.rem(target + 127, 128)
            if j < 4:
                up_a = jnp.where(mark, moved, up_a)
                low_a = jnp.where(low_mark, moved, low_a)
            else:
                up_b = jnp.where(mark, moved, up_b)
                low_b = jnp.where(low_mark, moved, low_b)
        return up_a, up_b, low_q, low_a, low_b

    nothing = jnp.zeros((16, 128), jnp.float32)
    up_a, up_b, low_q, low_a, low_b = lax.fori_loop(0, 8, pack, (nothing,) * 5)
    low_a = jnp.where(lane < 96, roll(low_q, 2), roll(low_a, 1))
    low_b = roll(low_b, 1)
    in_eight = lax.rem(lane, 8)
    for side, (a, b) in enumerate(((up_a, up_b), (low_a, low_b))):
        zt[2 * side] = a
        zt[2 * side + 1] = b
        zt[4 + side] = jnp.where(
            (in_eight < 2) | (in_eight >= 6), a, jnp.where(in_eight < 4, roll(b, 2), roll(b, -2))
        )

    for side in range(2):
        row = LO if side == 0 else HI - 1
        for k in range(6):
            member = Y_SET[side][k]
            ys[side, k] = ps[2:10, row, :] if member == PSI else pg[SLOT[member], 2:10, row, :]
    for side in range(2):
        for xs in range(2):
            for k in range(6):
                yx[2 * side + xs, 2 * k : 2 * k + 2, :] = ys[side, k, 6 * xs : 6 * xs + 2, :]
    pl.semaphore_wait(barrier, expected)
    for index, offset in enumerate(NEAR):
        other_elder, _ = ages(offset)

        @pl.when(other_elder == 1)
        def _():
            pl.semaphore_signal(ready.at[index], inc=1, device_id=at(offset), device_id_type=MESH_ID)


    def copy_to(offset, src, dst, sends, recvs, index):
        return pltpu.make_async_remote_copy(
            src_ref=src, dst_ref=dst, send_sem=sends.at[index], recv_sem=recvs.at[index],
            device_id=at(tuple(-o for o in offset)), device_id_type=MESH_ID,
        )

    def message(index, offset, src, dst):
        copy = copy_to(offset, src, dst, send, recv, index)
        by_offset[offset].append(copy)
        return copy

    z_copies, y_copies, x_copies = [], [], []
    by_offset = {offset: [] for offset in NEAR}
    block = pl.ds(LO, 16)
    for offset in NEAR:
        dx, dy, dz = offset
        if dz != 0:
            side = 0 if dz > 0 else 1
            if dx == 0:
                z_copies.append(message(side, offset, zt.at[pl.ds(2 * side, 2)], zz.at[pl.ds(2 * side, 2)]))
            else:
                xs = 0 if dx > 0 else 1
                z_copies.append(
                    message(2 + 2 * side + xs, offset, zt.at[4 + side], zz.at[4 + 2 * side + xs])
                )
    for xs in range(2):
        offset = (1 - 2 * xs, 0, 0)
        z_copies.append(message(6 + xs, offset, zt.at[pl.ds(4, 2)], zz.at[pl.ds(8 + 2 * xs, 2)]))
    for side in range(2):
        for xs in range(2):
            offset = (1 - 2 * xs, 1 - 2 * side, 0)
            y_copies.append(message(8 + 2 * side + xs, offset, yx.at[2 * side + xs], ye.at[2 * side + xs]))
        y_copies.append(message(12 + side, (0, 1 - 2 * side, 0), ys.at[side], yr.at[side]))
    for xs in range(2):
        offset = (1 - 2 * xs, 0, 0)
        if xs == 0:
            parts = ((pl.ds(0, 18), 2, 10), (pl.ds(0, 6), 3, 11))
        else:
            parts = ((pl.ds(6, 18), 9, 1), (pl.ds(18, 6), 8, 0))
        for k, (slots, near, far) in enumerate(parts):
            x_copies.append(
                message(14 + 2 * xs + k, offset, pg.at[slots, near, block, :], pg.at[slots, far, block, :])
            )
    for offset in NEAR:
        _, own_elder = ages(opposite(offset))

        @pl.when(own_elder == 0)
        def _():
            for copy in by_offset[offset]:
                copy.start()


    def span(start, count):
        return (lane >= start) & (lane < start + count)

    def place(value, tile, source, group, start, count, deep):
        mark = span(16 * group + start, count)
        if deep:
            mark = mark | span(16 * group + 16 + start, count)
        return jnp.where(mark, roll(tile, 16 * group + start - source), value)

    def fill(value, tiles, side, spot, group, deep):
        return place(value, tiles[2 * side + spot // 16], 8 * (spot % 16), group, 2, 8, deep)

    def fill_edges(value, own, side, spot, group, deep, cx):
        for xs, start, low, high in ((0, 10, 0, 2), (1, 0, 6, 4)):
            if cx is not None and cx == (-1 if xs == 0 else 1):
                continue
            tile = zz[8 + 2 * xs + side] if own else zz[4 + 2 * side + xs]
            source = 8 * (spot % 16) + (low if spot < 16 else high)
            value = place(value, tile, source, group, start, 2, deep)
        return value

    parts = []
    for j in range(5):
        parts.append((SLOT[UP[j]], DIRECTIONS[UP[j]][0], [(True, 0, QUAD[j], 2, True), (False, 0, QUAD[j], 6, True)]))
        parts.append((SLOT[DOWN[j]], DIRECTIONS[DOWN[j]][0], [(True, 1, QUAD[j], 4, True), (False, 1, QUAD[j], 0, True)]))
    for j in range(12):
        slot, cx = (SLOT[FLAT[j]], DIRECTIONS[FLAT[j]][0]) if j < 9 else (MOM + j - 9, None)
        parts.append((slot, cx, [
            (True, 0, 12 + j, 2, False), (True, 1, 12 + j, 5, False),
            (False, 0, 12 + j, 6, False), (False, 1, 12 + j, 1, False),
        ]))
    parts.append((RHO, None, [
        (True, 0, QUAD[5], 2, True), (True, 1, QUAD[5], 4, True),
        (False, 0, QUAD[5], 6, True), (False, 1, QUAD[5], 0, True),
    ]))

    for slot, _, pieces in parts:
        value = nothing
        for own_part, side, spot, group, deep in pieces:
            if own_part:
                value = fill(value, zt, side, spot, group, deep)
        strip[slot, LO:HI, :] = value

    def collide_pass(xi, carry):
        g = []
        for member in range(19):
            dx, dy, dz = DIRECTIONS[member]
            value = roll(pg[SLOT[member], xi + dx, LO + dy : HI + dy, :], -dz)
            g.append(value)
            hs[4 + member, xi] = (1.0 - OMEGA) * value
        psi, grad = gradient(
            lambda dx, dy: ps[xi + dx, LO + dy : HI + dy, :], lambda value: roll(value, -1), lambda value: roll(value, 1)
        )
        force_bar, h, base, near = collide(
            g, density[xi], [pg[MOM + c, xi, LO:HI, :] for c in range(3)], psi, grad
        )
        for c in range(3):
            fp[c, xi, LO:HI, :] = psi * force_bar[c]
            hs[1 + c, xi] = h[c]
        hs[0, xi] = base - COUPLING * ((1.0 - psi) * near)
        return carry

    near_y = y_copies[2::3]
    far_y = [copy for copy in y_copies if not any(copy is other for other in near_y)]
    for copy in near_y:
        copy.wait_recv()
    for side in range(2):
        row = HI if side == 0 else LO - 1
        for k in range(6):
            member = Y_SET[side][k]
            for start, count, value in ((2, 8, yr[side, k]),):
                if member == PSI:
                    ps[start : start + count, row, :] = value
                else:
                    pg[SLOT[member], start : start + count, row, :] = value
    lax.fori_loop(4, 8, collide_pass, 0)
    for index, offset in enumerate(NEAR):
        _, own_elder = ages(opposite(offset))

        @pl.when(own_elder == 1)
        def _():
            pl.semaphore_wait(ready.at[index], 1)
            for copy in by_offset[offset]:
                copy.start()

    for copy in z_copies:
        copy.wait_recv()
    for slot, cx, pieces in parts:
        value = strip[slot, LO:HI, :]
        for own_part, side, spot, group, deep in pieces:
            if not own_part:
                value = fill(value, zz, side, spot, group, deep)
            value = fill_edges(value, own_part, side, spot, group, deep, cx)
        strip[slot, LO:HI, :] = value
    sps[LO:HI, :] = 1.0 - jnp.exp(-strip[RHO, LO:HI, :])

    def strip_row(member):
        return sps if member == PSI else strip.at[SLOT[member]]

    def along_y(side, src, dst, index):
        return copy_to((0, 1 - 2 * side, 0), src, dst, send_y, recv_y, index)

    for side in range(2):
        row = LO if side == 0 else HI - 1
        for k in range(6):
            bs[side, k : k + 1, :] = strip_row(Y_SET[side][k])[row : row + 1, :]
    y_first = [along_y(side, bs.at[side], br.at[side], side) for side in range(2)]
    for copy in y_first:
        copy.start()
    for copy in far_y + x_copies:
        copy.wait_recv()
    for side in range(2):
        row = HI if side == 0 else LO - 1
        for k in range(6):
            member = Y_SET[side][k]
            for xs, start in ((0, 10), (1, 0)):
                value = ye[2 * side + xs, 2 * k : 2 * k + 2, :]
                if member == PSI:
                    ps[start : start + 2, row, :] = value
                else:
                    pg[SLOT[member], start : start + 2, row, :] = value
    for xi, slot in ((0, RHO2), (1, RHO2), (10, RHO), (11, RHO)):
        value = pg[slot, xi, LO:HI, :]
        density[xi] = value
        ps[xi, LO:HI, :] = 1.0 - jnp.exp(-value)
    lax.fori_loop(1, 4, collide_pass, 0)
    lax.fori_loop(8, 11, collide_pass, 0)
    for copy in y_first:
        copy.wait_recv()
    for side in range(2):
        row = HI if side == 0 else LO - 1
        for k in range(6):
            strip_row(Y_SET[side][k])[row : row + 1, :] = br[side, k : k + 1, :]

    g = []
    for member in range(19):
        dx, dy, dz = DIRECTIONS[member]
        g.append(roll(strip[SLOT[member], LO + dy : HI + dy, :], -(16 * dz + dx)))
    psi, grad = gradient(
        lambda dx, dy: roll(sps[LO + dy : HI + dy, :], -dx), lambda value: roll(value, -16), lambda value: roll(value, 16)
    )
    inside = span(17, 10) | span(33, 10) | span(81, 10) | span(97, 10)
    own_rho = jnp.where(inside, strip[RHO, LO:HI, :], 1.0)
    force_bar, h, base, near = collide(g, own_rho, [strip[MOM + c, LO:HI, :] for c in range(3)], psi, grad)
    for c in range(3):
        fs[c, LO:HI, :] = jnp.where(inside, psi * force_bar[c], 0.0)
        so[20 + c] = h[c]
    so[19] = base - COUPLING * ((1.0 - psi) * near)
    for member in range(19):
        so[member] = (1.0 - OMEGA) * g[member]

    def patch(xi, carry):
        for c in range(3):
            outer = fs[c, LO:HI, :]
            fp[c, xi, LO:HI, :] = jnp.where(
                upper, roll(outer, 47 - xi), jnp.where(lower, roll(outer, 96 - xi), fp[c, xi, LO:HI, :])
            )
        return carry

    lax.fori_loop(1, 11, patch, 0)
    beyond = lane >= 64

    def signed(value):
        return jnp.where(beyond, value, -value)

    fx, fz = fs[0, LO:HI, :], signed(fs[2, LO:HI, :])
    rs[...] = W1 * fz + W2 * (
        roll(fx + fz, -1) - roll(fx - fz, 1)
        + (fs[1, LO + 1 : HI + 1, :] + signed(fs[2, LO + 1 : HI + 1, :]))
        - (fs[1, LO - 1 : HI - 1, :] - signed(fs[2, LO - 1 : HI - 1, :]))
    )

    sub8 = lax.broadcasted_iota(jnp.int32, (8, 128), 0)
    for side in range(2):
        sign = 1.0 if side == 0 else -1.0
        row = LO if side == 0 else HI - 1

        def column(value, start):
            picked = jnp.where(lane8 == sub8 + start, jnp.broadcast_to(value, (8, 128)), 0.0)
            return jnp.sum(picked, axis=1, keepdims=True)

        fx_p, fx_m = fp[0, 3:11, row, :], fp[0, 1:9, row, :]
        fy_p, fy_m = fp[1, 3:11, row, :], fp[1, 1:9, row, :]
        fy, fz = sign * fp[1, 2:10, row, :], fp[2, 2:10, row, :]
        sy, sz = sign * fs[1, row : row + 1, :], fs[2, row : row + 1, :]
        over = jnp.where(lane8 == 127, column(sy + sz, 98), roll(fy + fz, -1))
        under = jnp.where(lane8 == 0, column(sy - sz, 18), roll(fy - fz, 1))
        cs[side] = W1 * fy + W2 * ((fx_p - fx_m) + sign * (fy_p + fy_m) + over + under)
    y_second = [along_y(side, cs.at[side], cr.at[side], 2 + side) for side in range(2)]
    for copy in y_second:
        copy.start()

    def combined(own_parts, base, h):
        plus = [base + c for c in h]
        minus = [base - c for c in h]
        outs = []
        for member in range(19):
            total = base
            for c, o in enumerate(DIRECTIONS[member]):
                if o != 0:
                    total = (plus[c] if o > 0 else minus[c]) if total is base else (
                        total + h[c] if o > 0 else total - h[c]
                    )
            outs.append(own_parts[member] + total)
        return outs

    for member, value in enumerate(combined([so[k] for k in range(19)], so[19], [so[20 + c] for c in range(3)])):
        so[member] = value

    def spread_pass(x, carry):
        xi = x + 2

        def cell(c, dx, dy):
            return fp[c, xi + dx, LO + dy : HI + dy, :]

        q = cell(0, 1, 0) - cell(0, -1, 0) + cell(1, 0, 1) - cell(1, 0, -1)
        r = cell(2, 1, 0) + cell(2, -1, 0) + cell(2, 0, 1) + cell(2, 0, -1)
        r = W1 * cell(2, 0, 0) + W2 * r
        corner = (
            (cell(0, 1, 1) + cell(1, 1, 1))
            - (cell(0, -1, -1) + cell(1, -1, -1))
            + (cell(0, 1, -1) - cell(1, 1, -1))
            - (cell(0, -1, 1) - cell(1, -1, 1))
        )
        q2 = W2 * q
        outer = rs[...]
        over = jnp.where(upper, roll(outer, 31 - xi), roll(q2 + r, -1))
        under = jnp.where(lower, roll(outer, 112 - xi), roll(q2 - r, 1))
        rl[x] = W1 * q + W2 * corner + over + under
        outs = combined([hs[4 + member, xi] for member in range(19)], hs[0, xi], [hs[1 + c, xi] for c in range(3)])
        for member in range(19):
            face = so[member]
            part_ref[member, x] = jnp.where(
                upper, roll(face, 47 - xi), jnp.where(lower, roll(face, 96 - xi), outs[member])
            )
        return carry

    lax.fori_loop(0, 8, spread_pass, 0)

    for copy in y_second:
        copy.wait_recv()
    rl[:, 15, :] = rl[:, 15, :] + cr[0]
    rl[:, 0, :] = rl[:, 0, :] + cr[1]
    term_ref[...] = COUPLING * dec[...] * rl[...]
    for copy in z_copies + y_copies + x_copies + y_first + y_second:
        copy.wait_send()


def per_device(populations, adjoint_next):
    f32 = jnp.float32
    dma = pltpu.SemaphoreType.DMA
    shapes = (
        (19, 8, 16, 128),
        (24, 12, 32, 128),
        (12, 32, 128),
        (12, 16, 128),
        (8, 16, 128),
        (6, 16, 128),
        (12, 16, 128),
        (24, 32, 128),
        (32, 128),
        (23, 16, 128),
        (3, 32, 128),
        (16, 128),
        (3, 12, 32, 128),
        (23, 12, 16, 128),
        (8, 16, 128),
        (2, 6, 8, 128),
        (2, 6, 8, 128),
        (4, 16, 128),
        (4, 16, 128),
        (2, 8, 128),
        (2, 8, 128),
        (2, 8, 128),
        (2, 8, 128),
    )
    part, term = pl.pallas_call(
        kernel,
        out_shape=[jax.ShapeDtypeStruct((19, 8, 16, 128), f32), jax.ShapeDtypeStruct((8, 16, 128), f32)],
        in_specs=[pl.BlockSpec(memory_space=pl.ANY)] * 2,
        out_specs=[pl.BlockSpec(memory_space=pltpu.VMEM)] * 2,
        scratch_shapes=[pltpu.VMEM(shape, f32) for shape in shapes]
        + [pltpu.SemaphoreType.REGULAR((14,)), dma((19,)), dma((19,)), dma((18,)), dma((18,)), dma((4,)), dma((4,))],
        compiler_params=pltpu.CompilerParams(
            collective_id=0, has_side_effects=True, vmem_limit_bytes=40 * 1024 * 1024
        ),
    )(
        pltpu.with_memory_space_constraint(populations, pltpu.HBM),
        pltpu.with_memory_space_constraint(adjoint_next, pltpu.HBM),
    )
    return part + term[None]


def solution(mesh):
    return jax.shard_map(
        per_device,
        mesh=mesh,
        in_specs=(P(None, "gx", "gy", "gz"), P(None, "gx", "gy", "gz")),
        out_specs=P(None, "gx", "gy", "gz"),
        check_vma=False,
    )
```

```python
import jax
import jax.numpy as jnp
from jax import lax
from jax.experimental import pallas as pl
from jax.experimental.pallas import tpu as pltpu
from jax.sharding import PartitionSpec as P

DIRECTIONS = (
    (0, 0, 0),
    (1, 0, 0),
    (-1, 0, 0),
    (0, 1, 0),
    (0, -1, 0),
    (0, 0, 1),
    (0, 0, -1),
    (1, 1, 0),
    (-1, -1, 0),
    (1, -1, 0),
    (-1, 1, 0),
    (1, 0, 1),
    (-1, 0, -1),
    (1, 0, -1),
    (-1, 0, 1),
    (0, 1, 1),
    (0, -1, -1),
    (0, 1, -1),
    (0, -1, 1),
)
W0, W1, W2 = 1.0 / 3.0, 1.0 / 18.0, 1.0 / 36.0
OMEGA = 1.0 / 0.8
KAPPA = 1.0 - 0.5 / 0.8
COUPLING = -5.5

X_PLUS = (1, 7, 9, 11, 13)
X_ZERO = (0, 3, 4, 5, 6, 15, 16, 17, 18)
X_MINUS = (2, 8, 10, 12, 14)
RHO, MOM, RHO2 = 5, 6, 18
SLOT = {}
for place, member in enumerate(X_PLUS):
    SLOT[member] = place
for place, member in enumerate(X_ZERO):
    SLOT[member] = 9 + place
for place, member in enumerate(X_MINUS):
    SLOT[member] = 19 + place
PSI = -1
Y_SET = ((3, 15, 17, 7, PSI, 10), (4, 16, 18, 9, PSI, 8))
UP = (5, 11, 14, 15, 18)
DOWN = (6, 13, 12, 17, 16)
FLAT = (0, 1, 2, 3, 4, 7, 8, 9, 10)
QUAD = (0, 1, 4, 5, 8, 9)
LO, HI = 8, 24
MESH_ID = pl.DeviceIdType.MESH
NEAR = (
    (0, 0, 1), (0, 0, -1), (1, 0, 1), (1, 0, -1), (-1, 0, 1), (-1, 0, -1),
    (1, 1, 0), (1, -1, 0), (-1, 1, 0), (-1, -1, 0), (0, 1, 0), (0, -1, 0), (1, 0, 0), (-1, 0, 0),
)


def roll(value, amount, axis=1):
    if isinstance(amount, int):
        amount = amount % value.shape[axis]
        if amount == 0:
            return value
    return pltpu.roll(value, amount, axis)


def collide(g, rho, mom, psi, grad):
    s = {i: g[i] + g[i + 1] for i in range(1, 19, 2)}
    d = {i: g[i] - g[i + 1] for i in range(1, 19, 2)}
    sxy, sxz, syz = s[7] + s[9], s[11] + s[13], s[15] + s[17]
    a = W0 * g[0] + W1 * (s[1] + s[3] + s[5]) + W2 * (sxy + sxz + syz)
    b = (
        3.0 * W1 * d[1] + 3.0 * W2 * ((d[7] + d[9]) + (d[11] + d[13])),
        3.0 * W1 * d[3] + 3.0 * W2 * ((d[7] - d[9]) + (d[15] + d[17])),
        3.0 * W1 * d[5] + 3.0 * W2 * ((d[11] - d[13]) + (d[15] - d[17])),
    )
    a3 = 3.0 * a
    txx = 9.0 * W1 * s[1] + 9.0 * W2 * (sxy + sxz) - a3
    tyy = 9.0 * W1 * s[3] + 9.0 * W2 * (sxy + syz) - a3
    tzz = 9.0 * W1 * s[5] + 9.0 * W2 * (sxz + syz) - a3
    txy = 9.0 * W2 * (s[7] - s[9])
    txz = 9.0 * W2 * (s[11] - s[13])
    tyz = 9.0 * W2 * (s[15] - s[17])
    inverse = 1.0 / rho
    strength = -COUPLING * psi
    force = [strength * c for c in grad]
    u = [(mom[c] + 0.5 * force[c]) * inverse for c in range(3)]
    accel = [c * inverse for c in force]

    def tensor(v):
        return (
            txx * v[0] + txy * v[1] + txz * v[2],
            txy * v[0] + tyy * v[1] + tyz * v[2],
            txz * v[0] + tyz * v[1] + tzz * v[2],
        )

    tu, w = tensor(u), tensor(accel)
    v = [b[c] + tu[c] for c in range(3)]
    force_bar = [v[c] + (0.5 * KAPPA) * w[c] for c in range(3)]
    h = [OMEGA * v[c] + KAPPA * w[c] for c in range(3)]
    e = a + 0.5 * (u[0] * (b[0] + v[0]) + u[1] * (b[1] + v[1]) + u[2] * (b[2] + v[2]))
    near = force_bar[0] * grad[0] + force_bar[1] * grad[1] + force_bar[2] * grad[2]
    base = OMEGA * e - (u[0] * h[0] + u[1] * h[1] + u[2] * h[2])
    return force_bar, h, base, near


def gradient(get, up, down):
    psi = get(0, 0)
    xp, xm, yp, ym = get(1, 0), get(-1, 0), get(0, 1), get(0, -1)
    along_x, along_y = xp - xm, yp - ym
    along_z = W1 * psi + W2 * (xp + xm + yp + ym)
    main, cross = get(1, 1) - get(-1, -1), get(1, -1) - get(-1, 1)
    grad = (
        W1 * along_x + W2 * ((main + cross) + (up(along_x) + down(along_x))),
        W1 * along_y + W2 * ((main - cross) + (up(along_y) + down(along_y))),
        up(along_z) - down(along_z),
    )
    return psi, grad


def kernel(pop_hbm, adj_hbm, part_ref, term_ref,
           pops, pg, ps, density, dec, zt, zz, strip, sps, so, fs, rs, fp, hs, rl,
           ys, yr, ye, yx, bs, br, cs, cr,
           ready, sem_pop, sem_adj, send, recv, send_y, recv_y):
    sizes = [lax.axis_size(name) for name in ("gx", "gy", "gz")]
    here = [lax.axis_index(name) for name in ("gx", "gy", "gz")]

    def at(offset):
        return tuple(lax.rem(h + o + n, n) for h, o, n in zip(here, offset, sizes))

    def ages(offset):
        (px, _, pz), (x, _, z) = at(offset), here
        half = sizes[2] // 2
        low, other_low = (z < half).astype(jnp.int32), (pz < half).astype(jnp.int32)
        wrap = (jnp.abs(px - x) > 1).astype(jnp.int32) * (low == other_low).astype(jnp.int32)
        other = other_low * (1 - low) + wrap * (px == 0).astype(jnp.int32)
        own = low * (1 - other_low) + wrap * (x == 0).astype(jnp.int32)
        return other, own

    def opposite(offset):
        return tuple(-o for o in offset)

    barrier = pltpu.get_barrier_semaphore()
    expected = 0
    for offset in NEAR:
        other_elder, own_elder = ages(offset)
        expected = expected + (1 - own_elder)

        @pl.when(other_elder == 0)
        def _():
            pl.semaphore_signal(barrier, inc=1, device_id=at(offset), device_id_type=MESH_ID)

    own = pl.ds(2, 8)
    pop_in = [
        pltpu.make_async_copy(pop_hbm.at[pl.ds(i, n)], pops.at[pl.ds(i, n)], sem_pop.at[i])
        for i, n in ((0, 5), (5, 5), (10, 5), (15, 4))
    ]
    adj_in = [
        pltpu.make_async_copy(
            adj_hbm.at[pl.ds(i, n)], pg.at[pl.ds(SLOT[i], n), own, pl.ds(LO, 16), :], sem_adj.at[i]
        )
        for i, n in ((0, 1), (1, 1), (2, 1), (3, 4), (7, 1), (8, 1), (9, 1), (10, 1), (11, 1), (12, 1), (13, 1), (14, 1), (15, 4))
    ]
    for copy in pop_in + adj_in:
        copy.start()
    pl.semaphore_wait(barrier, expected)
    for index, offset in enumerate(NEAR):
        other_elder, _ = ages(offset)

        @pl.when(other_elder == 1)
        def _():
            pl.semaphore_signal(ready.at[index], inc=1, device_id=at(offset), device_id_type=MESH_ID)

    lane = lax.broadcasted_iota(jnp.int32, (16, 128), 1)
    lane8 = lane[:8]
    upper, lower = lane == 127, lane == 0
    for ref in (sps, fs, strip, fp):
        ref[...] = jnp.zeros(ref.shape, jnp.float32)
    for copy in pop_in:
        copy.wait()

    def density_pass(x, carry):
        f = [pops[i, x] for i in range(19)]
        rho = f[0]
        for i in range(1, 19):
            rho = rho + f[i]
        decay = jnp.exp(-rho)
        pg[RHO, x + 2, LO:HI, :] = rho
        pg[RHO2, x + 2, LO:HI, :] = rho
        density[x + 2] = rho
        dec[x] = decay
        ps[x + 2, LO:HI, :] = 1.0 - decay
        d = {i: f[i] - f[i + 1] for i in range(1, 19, 2)}
        pg[MOM, x + 2, LO:HI, :] = d[1] + (d[7] + d[9]) + (d[11] + d[13])
        pg[MOM + 1, x + 2, LO:HI, :] = d[3] + (d[7] - d[9]) + (d[15] + d[17])
        pg[MOM + 2, x + 2, LO:HI, :] = d[5] + (d[11] - d[13]) + (d[15] - d[17])
        return carry

    lax.fori_loop(0, 8, density_pass, 0)
    for copy in adj_in:
        copy.wait()

    def pack(x, carry):
        up_a, up_b, low_q, low_a, low_b = carry

        def split(j):
            if j == 5:
                return pg[RHO, x + 2, LO:HI, :]
            return jnp.where(lane < 64, pg[SLOT[UP[j]], x + 2, LO:HI, :], pg[SLOT[DOWN[j]], x + 2, LO:HI, :])

        for j in range(6):
            value = split(j)
            for deeper in range(2):
                target = 8 * (QUAD[j] + 2 * deeper) + x
                moved = roll(value, lax.rem(target + 128 - deeper, 128))
                up_a = jnp.where(lane == target, moved, up_a)
                low_q = jnp.where(lane == lax.rem(target + 126, 128), moved, low_q)
        for j in range(12):
            value = pg[SLOT[FLAT[j]], x + 2, LO:HI, :] if j < 9 else pg[MOM + j - 9, x + 2, LO:HI, :]
            target = 8 * ((12 + j) % 16) + x
            moved = roll(value, target)
            mark, low_mark = lane == target, lane == lax.rem(target + 127, 128)
            if j < 4:
                up_a = jnp.where(mark, moved, up_a)
                low_a = jnp.where(low_mark, moved, low_a)
            else:
                up_b = jnp.where(mark, moved, up_b)
                low_b = jnp.where(low_mark, moved, low_b)
        return up_a, up_b, low_q, low_a, low_b

    nothing = jnp.zeros((16, 128), jnp.float32)
    up_a, up_b, low_q, low_a, low_b = lax.fori_loop(0, 8, pack, (nothing,) * 5)
    low_a = jnp.where(lane < 96, roll(low_q, 2), roll(low_a, 1))
    low_b = roll(low_b, 1)
    in_eight = lax.rem(lane, 8)
    for side, (a, b) in enumerate(((up_a, up_b), (low_a, low_b))):
        zt[2 * side] = a
        zt[2 * side + 1] = b
        zt[4 + side] = jnp.where(
            (in_eight < 2) | (in_eight >= 6), a, jnp.where(in_eight < 4, roll(b, 2), roll(b, -2))
        )

    for side in range(2):
        row = LO if side == 0 else HI - 1
        for k in range(6):
            member = Y_SET[side][k]
            ys[side, k] = ps[2:10, row, :] if member == PSI else pg[SLOT[member], 2:10, row, :]
    for side in range(2):
        for xs in range(2):
            for k in range(6):
                yx[2 * side + xs, 2 * k : 2 * k + 2, :] = ys[side, k, 6 * xs : 6 * xs + 2, :]
    def copy_to(offset, src, dst, sends, recvs, index):
        return pltpu.make_async_remote_copy(
            src_ref=src, dst_ref=dst, send_sem=sends.at[index], recv_sem=recvs.at[index],
            device_id=at(tuple(-o for o in offset)), device_id_type=MESH_ID,
        )

    def message(index, offset, src, dst):
        copy = copy_to(offset, src, dst, send, recv, index)
        by_offset[offset].append(copy)
        return copy

    z_copies, y_copies, x_copies = [], [], []
    by_offset = {offset: [] for offset in NEAR}
    block = pl.ds(LO, 16)
    for offset in NEAR:
        dx, dy, dz = offset
        if dz != 0:
            side = 0 if dz > 0 else 1
            if dx == 0:
                z_copies.append(message(side, offset, zt.at[pl.ds(2 * side, 2)], zz.at[pl.ds(2 * side, 2)]))
            else:
                xs = 0 if dx > 0 else 1
                z_copies.append(
                    message(2 + 2 * side + xs, offset, zt.at[4 + side], zz.at[4 + 2 * side + xs])
                )
    for xs in range(2):
        offset = (1 - 2 * xs, 0, 0)
        z_copies.append(message(6 + xs, offset, zt.at[pl.ds(4, 2)], zz.at[pl.ds(8 + 2 * xs, 2)]))
    for side in range(2):
        for xs in range(2):
            offset = (1 - 2 * xs, 1 - 2 * side, 0)
            y_copies.append(message(8 + 2 * side + xs, offset, yx.at[2 * side + xs], ye.at[2 * side + xs]))
        y_copies.append(message(12 + side, (0, 1 - 2 * side, 0), ys.at[side], yr.at[side]))
    for xs in range(2):
        offset = (1 - 2 * xs, 0, 0)
        if xs == 0:
            parts = ((pl.ds(0, 18), 2, 10), (pl.ds(0, 6), 3, 11))
        else:
            parts = ((pl.ds(6, 18), 9, 1), (pl.ds(18, 6), 8, 0))
        for k, (slots, near, far) in enumerate(parts):
            x_copies.append(
                message(14 + 2 * xs + k, offset, pg.at[slots, near, block, :], pg.at[slots, far, block, :])
            )
    for offset in NEAR:
        _, own_elder = ages(opposite(offset))

        @pl.when(own_elder == 0)
        def _():
            for copy in by_offset[offset]:
                copy.start()


    def span(start, count):
        return (lane >= start) & (lane < start + count)

    def place(value, tile, source, group, start, count, deep):
        mark = span(16 * group + start, count)
        if deep:
            mark = mark | span(16 * group + 16 + start, count)
        return jnp.where(mark, roll(tile, 16 * group + start - source), value)

    def fill(value, tiles, side, spot, group, deep):
        return place(value, tiles[2 * side + spot // 16], 8 * (spot % 16), group, 2, 8, deep)

    def fill_edges(value, own, side, spot, group, deep, cx):
        for xs, start, low, high in ((0, 10, 0, 2), (1, 0, 6, 4)):
            if cx is not None and cx == (-1 if xs == 0 else 1):
                continue
            tile = zz[8 + 2 * xs + side] if own else zz[4 + 2 * side + xs]
            source = 8 * (spot % 16) + (low if spot < 16 else high)
            value = place(value, tile, source, group, start, 2, deep)
        return value

    parts = []
    for j in range(5):
        parts.append((SLOT[UP[j]], DIRECTIONS[UP[j]][0], [(True, 0, QUAD[j], 2, True), (False, 0, QUAD[j], 6, True)]))
        parts.append((SLOT[DOWN[j]], DIRECTIONS[DOWN[j]][0], [(True, 1, QUAD[j], 4, True), (False, 1, QUAD[j], 0, True)]))
    for j in range(12):
        slot, cx = (SLOT[FLAT[j]], DIRECTIONS[FLAT[j]][0]) if j < 9 else (MOM + j - 9, None)
        parts.append((slot, cx, [
            (True, 0, 12 + j, 2, False), (True, 1, 12 + j, 5, False),
            (False, 0, 12 + j, 6, False), (False, 1, 12 + j, 1, False),
        ]))
    parts.append((RHO, None, [
        (True, 0, QUAD[5], 2, True), (True, 1, QUAD[5], 4, True),
        (False, 0, QUAD[5], 6, True), (False, 1, QUAD[5], 0, True),
    ]))

    for slot, _, pieces in parts:
        value = nothing
        for own_part, side, spot, group, deep in pieces:
            if own_part:
                value = fill(value, zt, side, spot, group, deep)
        strip[slot, LO:HI, :] = value

    def collide_pass(xi, carry):
        g = []
        for member in range(19):
            dx, dy, dz = DIRECTIONS[member]
            value = roll(pg[SLOT[member], xi + dx, LO + dy : HI + dy, :], -dz)
            g.append(value)
            hs[4 + member, xi] = (1.0 - OMEGA) * value
        psi, grad = gradient(
            lambda dx, dy: ps[xi + dx, LO + dy : HI + dy, :], lambda value: roll(value, -1), lambda value: roll(value, 1)
        )
        force_bar, h, base, near = collide(
            g, density[xi], [pg[MOM + c, xi, LO:HI, :] for c in range(3)], psi, grad
        )
        for c in range(3):
            fp[c, xi, LO:HI, :] = psi * force_bar[c]
            hs[1 + c, xi] = h[c]
        hs[0, xi] = base - COUPLING * ((1.0 - psi) * near)
        return carry

    near_y = y_copies[2::3]
    far_y = [copy for copy in y_copies if not any(copy is other for other in near_y)]
    for copy in near_y:
        copy.wait_recv()
    for side in range(2):
        row = HI if side == 0 else LO - 1
        for k in range(6):
            member = Y_SET[side][k]
            for start, count, value in ((2, 8, yr[side, k]),):
                if member == PSI:
                    ps[start : start + count, row, :] = value
                else:
                    pg[SLOT[member], start : start + count, row, :] = value
    lax.fori_loop(3, 9, collide_pass, 0)
    for index, offset in enumerate(NEAR):
        _, own_elder = ages(opposite(offset))

        @pl.when(own_elder == 1)
        def _():
            pl.semaphore_wait(ready.at[index], 1)
            for copy in by_offset[offset]:
                copy.start()

    for copy in z_copies:
        copy.wait_recv()
    for slot, cx, pieces in parts:
        value = strip[slot, LO:HI, :]
        for own_part, side, spot, group, deep in pieces:
            if not own_part:
                value = fill(value, zz, side, spot, group, deep)
            value = fill_edges(value, own_part, side, spot, group, deep, cx)
        strip[slot, LO:HI, :] = value
    sps[LO:HI, :] = 1.0 - jnp.exp(-strip[RHO, LO:HI, :])

    def strip_row(member):
        return sps if member == PSI else strip.at[SLOT[member]]

    def along_y(side, src, dst, index):
        return copy_to((0, 1 - 2 * side, 0), src, dst, send_y, recv_y, index)

    for side in range(2):
        row = LO if side == 0 else HI - 1
        for k in range(6):
            bs[side, k : k + 1, :] = strip_row(Y_SET[side][k])[row : row + 1, :]
    y_first = [along_y(side, bs.at[side], br.at[side], side) for side in range(2)]
    for copy in y_first:
        copy.start()
    for copy in far_y + x_copies:
        copy.wait_recv()
    for side in range(2):
        row = HI if side == 0 else LO - 1
        for k in range(6):
            member = Y_SET[side][k]
            for xs, start in ((0, 10), (1, 0)):
                value = ye[2 * side + xs, 2 * k : 2 * k + 2, :]
                if member == PSI:
                    ps[start : start + 2, row, :] = value
                else:
                    pg[SLOT[member], start : start + 2, row, :] = value
    for xi, slot in ((0, RHO2), (1, RHO2), (10, RHO), (11, RHO)):
        value = pg[slot, xi, LO:HI, :]
        density[xi] = value
        ps[xi, LO:HI, :] = 1.0 - jnp.exp(-value)
    lax.fori_loop(1, 3, collide_pass, 0)
    lax.fori_loop(9, 11, collide_pass, 0)
    for copy in y_first:
        copy.wait_recv()
    for side in range(2):
        row = HI if side == 0 else LO - 1
        for k in range(6):
            strip_row(Y_SET[side][k])[row : row + 1, :] = br[side, k : k + 1, :]

    g = []
    for member in range(19):
        dx, dy, dz = DIRECTIONS[member]
        g.append(roll(strip[SLOT[member], LO + dy : HI + dy, :], -(16 * dz + dx)))
    psi, grad = gradient(
        lambda dx, dy: roll(sps[LO + dy : HI + dy, :], -dx), lambda value: roll(value, -16), lambda value: roll(value, 16)
    )
    inside = span(17, 10) | span(33, 10) | span(81, 10) | span(97, 10)
    own_rho = jnp.where(inside, strip[RHO, LO:HI, :], 1.0)
    force_bar, h, base, near = collide(g, own_rho, [strip[MOM + c, LO:HI, :] for c in range(3)], psi, grad)
    for c in range(3):
        fs[c, LO:HI, :] = jnp.where(inside, psi * force_bar[c], 0.0)
        so[20 + c] = h[c]
    so[19] = base - COUPLING * ((1.0 - psi) * near)
    for member in range(19):
        so[member] = (1.0 - OMEGA) * g[member]

    def patch(xi, carry):
        for c in range(3):
            outer = fs[c, LO:HI, :]
            fp[c, xi, LO:HI, :] = jnp.where(
                upper, roll(outer, 47 - xi), jnp.where(lower, roll(outer, 96 - xi), fp[c, xi, LO:HI, :])
            )
        return carry

    lax.fori_loop(1, 11, patch, 0)
    beyond = lane >= 64

    def signed(value):
        return jnp.where(beyond, value, -value)

    fx, fz = fs[0, LO:HI, :], signed(fs[2, LO:HI, :])
    rs[...] = W1 * fz + W2 * (
        roll(fx + fz, -1) - roll(fx - fz, 1)
        + (fs[1, LO + 1 : HI + 1, :] + signed(fs[2, LO + 1 : HI + 1, :]))
        - (fs[1, LO - 1 : HI - 1, :] - signed(fs[2, LO - 1 : HI - 1, :]))
    )

    sub8 = lax.broadcasted_iota(jnp.int32, (8, 128), 0)
    for side in range(2):
        sign = 1.0 if side == 0 else -1.0
        row = LO if side == 0 else HI - 1

        def column(value, start):
            picked = jnp.where(lane8 == sub8 + start, jnp.broadcast_to(value, (8, 128)), 0.0)
            return jnp.sum(picked, axis=1, keepdims=True)

        fx_p, fx_m = fp[0, 3:11, row, :], fp[0, 1:9, row, :]
        fy_p, fy_m = fp[1, 3:11, row, :], fp[1, 1:9, row, :]
        fy, fz = sign * fp[1, 2:10, row, :], fp[2, 2:10, row, :]
        sy, sz = sign * fs[1, row : row + 1, :], fs[2, row : row + 1, :]
        over = jnp.where(lane8 == 127, column(sy + sz, 98), roll(fy + fz, -1))
        under = jnp.where(lane8 == 0, column(sy - sz, 18), roll(fy - fz, 1))
        cs[side] = W1 * fy + W2 * ((fx_p - fx_m) + sign * (fy_p + fy_m) + over + under)
    y_second = [along_y(side, cs.at[side], cr.at[side], 2 + side) for side in range(2)]
    for copy in y_second:
        copy.start()

    def combined(own_parts, base, h):
        plus = [base + c for c in h]
        minus = [base - c for c in h]
        outs = []
        for member in range(19):
            total = base
            for c, o in enumerate(DIRECTIONS[member]):
                if o != 0:
                    total = (plus[c] if o > 0 else minus[c]) if total is base else (
                        total + h[c] if o > 0 else total - h[c]
                    )
            outs.append(own_parts[member] + total)
        return outs

    for member, value in enumerate(combined([so[k] for k in range(19)], so[19], [so[20 + c] for c in range(3)])):
        so[member] = value

    def spread_pass(x, carry):
        xi = x + 2

        def cell(c, dx, dy):
            return fp[c, xi + dx, LO + dy : HI + dy, :]

        q = cell(0, 1, 0) - cell(0, -1, 0) + cell(1, 0, 1) - cell(1, 0, -1)
        r = cell(2, 1, 0) + cell(2, -1, 0) + cell(2, 0, 1) + cell(2, 0, -1)
        r = W1 * cell(2, 0, 0) + W2 * r
        corner = (
            (cell(0, 1, 1) + cell(1, 1, 1))
            - (cell(0, -1, -1) + cell(1, -1, -1))
            + (cell(0, 1, -1) - cell(1, 1, -1))
            - (cell(0, -1, 1) - cell(1, -1, 1))
        )
        q2 = W2 * q
        outer = rs[...]
        over = jnp.where(upper, roll(outer, 31 - xi), roll(q2 + r, -1))
        under = jnp.where(lower, roll(outer, 112 - xi), roll(q2 - r, 1))
        rl[x] = W1 * q + W2 * corner + over + under
        outs = combined([hs[4 + member, xi] for member in range(19)], hs[0, xi], [hs[1 + c, xi] for c in range(3)])
        for member in range(19):
            face = so[member]
            part_ref[member, x] = jnp.where(
                upper, roll(face, 47 - xi), jnp.where(lower, roll(face, 96 - xi), outs[member])
            )
        return carry

    lax.fori_loop(0, 8, spread_pass, 0)

    for copy in y_second:
        copy.wait_recv()
    rl[:, 15, :] = rl[:, 15, :] + cr[0]
    rl[:, 0, :] = rl[:, 0, :] + cr[1]
    term_ref[...] = COUPLING * dec[...] * rl[...]
    for copy in z_copies + y_copies + x_copies + y_first + y_second:
        copy.wait_send()


def per_device(populations, adjoint_next):
    f32 = jnp.float32
    dma = pltpu.SemaphoreType.DMA
    shapes = (
        (19, 8, 16, 128),
        (24, 12, 32, 128),
        (12, 32, 128),
        (12, 16, 128),
        (8, 16, 128),
        (6, 16, 128),
        (12, 16, 128),
        (24, 32, 128),
        (32, 128),
        (23, 16, 128),
        (3, 32, 128),
        (16, 128),
        (3, 12, 32, 128),
        (23, 12, 16, 128),
        (8, 16, 128),
        (2, 6, 8, 128),
        (2, 6, 8, 128),
        (4, 16, 128),
        (4, 16, 128),
        (2, 8, 128),
        (2, 8, 128),
        (2, 8, 128),
        (2, 8, 128),
    )
    part, term = pl.pallas_call(
        kernel,
        out_shape=[jax.ShapeDtypeStruct((19, 8, 16, 128), f32), jax.ShapeDtypeStruct((8, 16, 128), f32)],
        in_specs=[pl.BlockSpec(memory_space=pl.ANY)] * 2,
        out_specs=[pl.BlockSpec(memory_space=pltpu.VMEM)] * 2,
        scratch_shapes=[pltpu.VMEM(shape, f32) for shape in shapes]
        + [pltpu.SemaphoreType.REGULAR((14,)), dma((19,)), dma((19,)), dma((18,)), dma((18,)), dma((4,)), dma((4,))],
        compiler_params=pltpu.CompilerParams(
            collective_id=0, has_side_effects=True, vmem_limit_bytes=40 * 1024 * 1024
        ),
    )(
        pltpu.with_memory_space_constraint(populations, pltpu.HBM),
        pltpu.with_memory_space_constraint(adjoint_next, pltpu.HBM),
    )
    return part + term[None]


def solution(mesh):
    return jax.shard_map(
        per_device,
        mesh=mesh,
        in_specs=(P(None, "gx", "gy", "gz"), P(None, "gx", "gy", "gz")),
        out_specs=P(None, "gx", "gy", "gz"),
        check_vma=False,
    )
```

```python
import jax
import jax.numpy as jnp
from jax import lax
from jax.experimental import pallas as pl
from jax.experimental.pallas import tpu as pltpu
from jax.sharding import PartitionSpec as P

DIRECTIONS = (
    (0, 0, 0),
    (1, 0, 0),
    (-1, 0, 0),
    (0, 1, 0),
    (0, -1, 0),
    (0, 0, 1),
    (0, 0, -1),
    (1, 1, 0),
    (-1, -1, 0),
    (1, -1, 0),
    (-1, 1, 0),
    (1, 0, 1),
    (-1, 0, -1),
    (1, 0, -1),
    (-1, 0, 1),
    (0, 1, 1),
    (0, -1, -1),
    (0, 1, -1),
    (0, -1, 1),
)
W0, W1, W2 = 1.0 / 3.0, 1.0 / 18.0, 1.0 / 36.0
OMEGA = 1.0 / 0.8
KAPPA = 1.0 - 0.5 / 0.8
COUPLING = -5.5

X_PLUS = (1, 7, 9, 11, 13)
X_ZERO = (0, 3, 4, 5, 6, 15, 16, 17, 18)
X_MINUS = (2, 8, 10, 12, 14)
RHO, MOM, RHO2 = 5, 6, 18
SLOT = {}
for place, member in enumerate(X_PLUS):
    SLOT[member] = place
for place, member in enumerate(X_ZERO):
    SLOT[member] = 9 + place
for place, member in enumerate(X_MINUS):
    SLOT[member] = 19 + place
PSI = -1
Y_SET = ((3, 15, 17, 7, PSI, 10), (4, 16, 18, 9, PSI, 8))
UP = (5, 11, 14, 15, 18)
DOWN = (6, 13, 12, 17, 16)
FLAT = (0, 1, 2, 3, 4, 7, 8, 9, 10)
QUAD = (0, 1, 4, 5, 8, 9)
LO, HI = 8, 24
MESH_ID = pl.DeviceIdType.MESH
NEAR = (
    (0, 0, 1), (0, 0, -1), (1, 0, 1), (1, 0, -1), (-1, 0, 1), (-1, 0, -1),
    (1, 1, 0), (1, -1, 0), (-1, 1, 0), (-1, -1, 0), (0, 1, 0), (0, -1, 0), (1, 0, 0), (-1, 0, 0),
)


def roll(value, amount, axis=1):
    if isinstance(amount, int):
        amount = amount % value.shape[axis]
        if amount == 0:
            return value
    return pltpu.roll(value, amount, axis)


def collide(g, rho, mom, psi, grad):
    s = {i: g[i] + g[i + 1] for i in range(1, 19, 2)}
    d = {i: g[i] - g[i + 1] for i in range(1, 19, 2)}
    sxy, sxz, syz = s[7] + s[9], s[11] + s[13], s[15] + s[17]
    a = W0 * g[0] + W1 * (s[1] + s[3] + s[5]) + W2 * (sxy + sxz + syz)
    b = (
        3.0 * W1 * d[1] + 3.0 * W2 * ((d[7] + d[9]) + (d[11] + d[13])),
        3.0 * W1 * d[3] + 3.0 * W2 * ((d[7] - d[9]) + (d[15] + d[17])),
        3.0 * W1 * d[5] + 3.0 * W2 * ((d[11] - d[13]) + (d[15] - d[17])),
    )
    a3 = 3.0 * a
    txx = 9.0 * W1 * s[1] + 9.0 * W2 * (sxy + sxz) - a3
    tyy = 9.0 * W1 * s[3] + 9.0 * W2 * (sxy + syz) - a3
    tzz = 9.0 * W1 * s[5] + 9.0 * W2 * (sxz + syz) - a3
    txy = 9.0 * W2 * (s[7] - s[9])
    txz = 9.0 * W2 * (s[11] - s[13])
    tyz = 9.0 * W2 * (s[15] - s[17])
    inverse = 1.0 / rho
    strength = -COUPLING * psi
    force = [strength * c for c in grad]
    u = [(mom[c] + 0.5 * force[c]) * inverse for c in range(3)]
    accel = [c * inverse for c in force]

    def tensor(v):
        return (
            txx * v[0] + txy * v[1] + txz * v[2],
            txy * v[0] + tyy * v[1] + tyz * v[2],
            txz * v[0] + tyz * v[1] + tzz * v[2],
        )

    tu, w = tensor(u), tensor(accel)
    v = [b[c] + tu[c] for c in range(3)]
    force_bar = [v[c] + (0.5 * KAPPA) * w[c] for c in range(3)]
    h = [OMEGA * v[c] + KAPPA * w[c] for c in range(3)]
    e = a + 0.5 * (u[0] * (b[0] + v[0]) + u[1] * (b[1] + v[1]) + u[2] * (b[2] + v[2]))
    near = force_bar[0] * grad[0] + force_bar[1] * grad[1] + force_bar[2] * grad[2]
    base = OMEGA * e - (u[0] * h[0] + u[1] * h[1] + u[2] * h[2])
    return force_bar, h, base, near


def gradient(get, up, down):
    psi = get(0, 0)
    xp, xm, yp, ym = get(1, 0), get(-1, 0), get(0, 1), get(0, -1)
    along_x, along_y = xp - xm, yp - ym
    along_z = W1 * psi + W2 * (xp + xm + yp + ym)
    main, cross = get(1, 1) - get(-1, -1), get(1, -1) - get(-1, 1)
    grad = (
        W1 * along_x + W2 * ((main + cross) + (up(along_x) + down(along_x))),
        W1 * along_y + W2 * ((main - cross) + (up(along_y) + down(along_y))),
        up(along_z) - down(along_z),
    )
    return psi, grad


def kernel(pop_hbm, adj_hbm, part_ref, term_ref,
           pops, pg, ps, density, dec, zt, zf, ze, rf, re, ro, zz, strip, sps, so, fs, rs, fp, hs, rl,
           ys, yr, ye, yx, bs, br, cs, cr,
           ready, sem_pop, sem_adj, send, recv, send_y, recv_y):
    sizes = [lax.axis_size(name) for name in ("gx", "gy", "gz")]
    here = [lax.axis_index(name) for name in ("gx", "gy", "gz")]

    def at(offset):
        return tuple(lax.rem(h + o + n, n) for h, o, n in zip(here, offset, sizes))

    def ages(offset):
        (px, _, pz), (x, _, z) = at(offset), here
        half = sizes[2] // 2
        low, other_low = (z < half).astype(jnp.int32), (pz < half).astype(jnp.int32)
        wrap = (jnp.abs(px - x) > 1).astype(jnp.int32) * (low == other_low).astype(jnp.int32)
        other = other_low * (1 - low) + wrap * (px == 0).astype(jnp.int32)
        own = low * (1 - other_low) + wrap * (x == 0).astype(jnp.int32)
        return other, own

    def opposite(offset):
        return tuple(-o for o in offset)

    barrier = pltpu.get_barrier_semaphore()
    expected = 0
    for offset in NEAR:
        other_elder, own_elder = ages(offset)
        expected = expected + (1 - own_elder)

        @pl.when(other_elder == 0)
        def _():
            pl.semaphore_signal(barrier, inc=1, device_id=at(offset), device_id_type=MESH_ID)

    own = pl.ds(2, 8)
    pop_in = [
        pltpu.make_async_copy(pop_hbm.at[pl.ds(i, n)], pops.at[pl.ds(i, n)], sem_pop.at[i])
        for i, n in ((0, 5), (5, 5), (10, 5), (15, 4))
    ]
    adj_in = [
        pltpu.make_async_copy(
            adj_hbm.at[pl.ds(i, n)], pg.at[pl.ds(SLOT[i], n), own, pl.ds(LO, 16), :], sem_adj.at[i]
        )
        for i, n in ((0, 1), (1, 1), (2, 1), (3, 4), (7, 1), (8, 1), (9, 1), (10, 1), (11, 1), (12, 1), (13, 1), (14, 1), (15, 4))
    ]
    for copy in pop_in + adj_in:
        copy.start()
    pl.semaphore_wait(barrier, expected)
    for index, offset in enumerate(NEAR):
        other_elder, _ = ages(offset)

        @pl.when(other_elder == 1)
        def _():
            pl.semaphore_signal(ready.at[index], inc=1, device_id=at(offset), device_id_type=MESH_ID)

    lane = lax.broadcasted_iota(jnp.int32, (16, 128), 1)
    lane8 = lane[:8]
    upper, lower = lane == 127, lane == 0
    for ref in (sps, fs, strip, fp):
        ref[...] = jnp.zeros(ref.shape, jnp.float32)
    for copy in pop_in:
        copy.wait()

    def density_pass(x, carry):
        f = [pops[i, x] for i in range(19)]
        rho = f[0]
        for i in range(1, 19):
            rho = rho + f[i]
        decay = jnp.exp(-rho)
        pg[RHO, x + 2, LO:HI, :] = rho
        pg[RHO2, x + 2, LO:HI, :] = rho
        density[x + 2] = rho
        dec[x] = decay
        ps[x + 2, LO:HI, :] = 1.0 - decay
        d = {i: f[i] - f[i + 1] for i in range(1, 19, 2)}
        pg[MOM, x + 2, LO:HI, :] = d[1] + (d[7] + d[9]) + (d[11] + d[13])
        pg[MOM + 1, x + 2, LO:HI, :] = d[3] + (d[7] - d[9]) + (d[15] + d[17])
        pg[MOM + 2, x + 2, LO:HI, :] = d[5] + (d[11] - d[13]) + (d[15] - d[17])
        return carry

    lax.fori_loop(0, 8, density_pass, 0)
    for copy in adj_in:
        copy.wait()

    def pack(x, carry):
        up_a, up_b, low_q, low_a, low_b = carry

        def split(j):
            if j == 5:
                return pg[RHO, x + 2, LO:HI, :]
            return jnp.where(lane < 64, pg[SLOT[UP[j]], x + 2, LO:HI, :], pg[SLOT[DOWN[j]], x + 2, LO:HI, :])

        for j in range(6):
            value = split(j)
            for deeper in range(2):
                target = 8 * (QUAD[j] + 2 * deeper) + x
                moved = roll(value, lax.rem(target + 128 - deeper, 128))
                up_a = jnp.where(lane == target, moved, up_a)
                low_q = jnp.where(lane == lax.rem(target + 126, 128), moved, low_q)
        for j in range(12):
            value = pg[SLOT[FLAT[j]], x + 2, LO:HI, :] if j < 9 else pg[MOM + j - 9, x + 2, LO:HI, :]
            target = 8 * ((12 + j) % 16) + x
            moved = roll(value, target)
            mark, low_mark = lane == target, lane == lax.rem(target + 127, 128)
            if j < 4:
                up_a = jnp.where(mark, moved, up_a)
                low_a = jnp.where(low_mark, moved, low_a)
            else:
                up_b = jnp.where(mark, moved, up_b)
                low_b = jnp.where(low_mark, moved, low_b)
        return up_a, up_b, low_q, low_a, low_b

    nothing = jnp.zeros((16, 128), jnp.float32)
    up_a, up_b, low_q, low_a, low_b = lax.fori_loop(0, 8, pack, (nothing,) * 5)
    low_a = jnp.where(lane < 96, roll(low_q, 2), roll(low_a, 1))
    low_b = roll(low_b, 1)
    in_eight = lax.rem(lane, 8)
    for side, (a, b) in enumerate(((up_a, up_b), (low_a, low_b))):
        zt[2 * side] = a
        zt[2 * side + 1] = b
        edge = jnp.where(
            (in_eight < 2) | (in_eight >= 6), a, jnp.where(in_eight < 4, roll(b, 2), roll(b, -2))
        )
        zf[side, 0] = a[:8]
        zf[side, 1] = a[8:]
        zf[side, 2] = jnp.where(lane8 < 64, b[:8], roll(b[8:], 64))
        ze[0, side] = jnp.where(in_eight[:8] < 4, edge[:8], roll(edge[8:], 4))
        ze[1, side] = jnp.where(in_eight[:8] >= 4, edge[:8], roll(edge[8:], -4))

    for side in range(2):
        row = LO if side == 0 else HI - 1
        for k in range(6):
            member = Y_SET[side][k]
            ys[side, k] = ps[2:10, row, :] if member == PSI else pg[SLOT[member], 2:10, row, :]
    for side in range(2):
        for xs in range(2):
            for k in range(6):
                yx[2 * side + xs, 2 * k : 2 * k + 2, :] = ys[side, k, 6 * xs : 6 * xs + 2, :]
    def copy_to(offset, src, dst, sends, recvs, index):
        return pltpu.make_async_remote_copy(
            src_ref=src, dst_ref=dst, send_sem=sends.at[index], recv_sem=recvs.at[index],
            device_id=at(tuple(-o for o in offset)), device_id_type=MESH_ID,
        )

    def message(index, offset, src, dst):
        copy = copy_to(offset, src, dst, send, recv, index)
        by_offset[offset].append(copy)
        return copy

    z_copies, y_copies, x_copies = [], [], []
    by_offset = {offset: [] for offset in NEAR}
    block = pl.ds(LO, 16)
    for offset in NEAR:
        dx, dy, dz = offset
        if dz != 0:
            side = 0 if dz > 0 else 1
            if dx == 0:
                z_copies.append(message(side, offset, zf.at[side], rf.at[side]))
            else:
                xs = 0 if dx > 0 else 1
                z_copies.append(
                    message(2 + 2 * side + xs, offset, ze.at[xs, side], re.at[2 * side + xs])
                )
    for xs in range(2):
        offset = (1 - 2 * xs, 0, 0)
        z_copies.append(message(6 + xs, offset, ze.at[xs], ro.at[xs]))
    for side in range(2):
        for xs in range(2):
            offset = (1 - 2 * xs, 1 - 2 * side, 0)
            y_copies.append(message(8 + 2 * side + xs, offset, yx.at[2 * side + xs], ye.at[2 * side + xs]))
        y_copies.append(message(12 + side, (0, 1 - 2 * side, 0), ys.at[side], yr.at[side]))
    for xs in range(2):
        offset = (1 - 2 * xs, 0, 0)
        if xs == 0:
            parts = ((pl.ds(0, 18), 2, 10), (pl.ds(0, 6), 3, 11))
        else:
            parts = ((pl.ds(6, 18), 9, 1), (pl.ds(18, 6), 8, 0))
        for k, (slots, near, far) in enumerate(parts):
            x_copies.append(
                message(14 + 2 * xs + k, offset, pg.at[slots, near, block, :], pg.at[slots, far, block, :])
            )
    for offset in NEAR:
        _, own_elder = ages(opposite(offset))

        @pl.when(own_elder == 0)
        def _():
            for copy in by_offset[offset]:
                copy.start()


    def span(start, count):
        return (lane >= start) & (lane < start + count)

    def place(value, tile, source, group, start, count, deep):
        mark = span(16 * group + start, count)
        if deep:
            mark = mark | span(16 * group + 16 + start, count)
        return jnp.where(mark, roll(tile, 16 * group + start - source), value)

    def fill(value, tiles, side, spot, group, deep):
        return place(value, tiles[2 * side + spot // 16], 8 * (spot % 16), group, 2, 8, deep)

    def fill_edges(value, own, side, spot, group, deep, cx):
        for xs, start, low, high in ((0, 10, 0, 2), (1, 0, 6, 4)):
            if cx is not None and cx == (-1 if xs == 0 else 1):
                continue
            tile = zz[8 + 2 * xs + side] if own else zz[4 + 2 * side + xs]
            source = 8 * (spot % 16) + (low if spot < 16 else high)
            value = place(value, tile, source, group, start, 2, deep)
        return value

    parts = []
    for j in range(5):
        parts.append((SLOT[UP[j]], DIRECTIONS[UP[j]][0], [(True, 0, QUAD[j], 2, True), (False, 0, QUAD[j], 6, True)]))
        parts.append((SLOT[DOWN[j]], DIRECTIONS[DOWN[j]][0], [(True, 1, QUAD[j], 4, True), (False, 1, QUAD[j], 0, True)]))
    for j in range(12):
        slot, cx = (SLOT[FLAT[j]], DIRECTIONS[FLAT[j]][0]) if j < 9 else (MOM + j - 9, None)
        parts.append((slot, cx, [
            (True, 0, 12 + j, 2, False), (True, 1, 12 + j, 5, False),
            (False, 0, 12 + j, 6, False), (False, 1, 12 + j, 1, False),
        ]))
    parts.append((RHO, None, [
        (True, 0, QUAD[5], 2, True), (True, 1, QUAD[5], 4, True),
        (False, 0, QUAD[5], 6, True), (False, 1, QUAD[5], 0, True),
    ]))

    for slot, _, pieces in parts:
        value = nothing
        for own_part, side, spot, group, deep in pieces:
            if own_part:
                value = fill(value, zt, side, spot, group, deep)
        strip[slot, LO:HI, :] = value

    def collide_pass(xi, carry):
        g = []
        for member in range(19):
            dx, dy, dz = DIRECTIONS[member]
            value = roll(pg[SLOT[member], xi + dx, LO + dy : HI + dy, :], -dz)
            g.append(value)
            hs[4 + member, xi] = (1.0 - OMEGA) * value
        psi, grad = gradient(
            lambda dx, dy: ps[xi + dx, LO + dy : HI + dy, :], lambda value: roll(value, -1), lambda value: roll(value, 1)
        )
        force_bar, h, base, near = collide(
            g, density[xi], [pg[MOM + c, xi, LO:HI, :] for c in range(3)], psi, grad
        )
        for c in range(3):
            fp[c, xi, LO:HI, :] = psi * force_bar[c]
            hs[1 + c, xi] = h[c]
        hs[0, xi] = base - COUPLING * ((1.0 - psi) * near)
        return carry

    near_y = y_copies[2::3]
    far_y = [copy for copy in y_copies if not any(copy is other for other in near_y)]
    for copy in near_y:
        copy.wait_recv()
    for side in range(2):
        row = HI if side == 0 else LO - 1
        for k in range(6):
            member = Y_SET[side][k]
            for start, count, value in ((2, 8, yr[side, k]),):
                if member == PSI:
                    ps[start : start + count, row, :] = value
                else:
                    pg[SLOT[member], start : start + count, row, :] = value
    lax.fori_loop(3, 9, collide_pass, 0)
    for index, offset in enumerate(NEAR):
        _, own_elder = ages(opposite(offset))

        @pl.when(own_elder == 1)
        def _():
            pl.semaphore_wait(ready.at[index], 1)
            for copy in by_offset[offset]:
                copy.start()

    for copy in z_copies:
        copy.wait_recv()
    for side in range(2):
        zz[2 * side, 0:8, :] = rf[side, 0]
        zz[2 * side, 8:16, :] = rf[side, 1]
        zz[2 * side + 1, 0:8, :] = rf[side, 2]
        zz[2 * side + 1, 8:16, :] = roll(rf[side, 2], 64)
        for xs in range(2):
            for target, tile in ((4 + 2 * side + xs, re[2 * side + xs]), (8 + 2 * xs + side, ro[xs, side])):
                zz[target, 0:8, :] = tile
                zz[target, 8:16, :] = roll(tile, -4 if xs == 0 else 4)
    def far_fill(wanted):
        for slot, cx, pieces in parts:
            if wanted != (slot in urgent):
                continue
            value = strip[slot, LO:HI, :]
            for own_part, side, spot, group, deep in pieces:
                if not own_part:
                    value = fill(value, zz, side, spot, group, deep)
                value = fill_edges(value, own_part, side, spot, group, deep, cx)
            strip[slot, LO:HI, :] = value

    urgent = {RHO} | {SLOT[member] for side in range(2) for member in Y_SET[side] if member != PSI}
    far_fill(True)
    sps[LO:HI, :] = 1.0 - jnp.exp(-strip[RHO, LO:HI, :])

    def strip_row(member):
        return sps if member == PSI else strip.at[SLOT[member]]

    def along_y(side, src, dst, index):
        return copy_to((0, 1 - 2 * side, 0), src, dst, send_y, recv_y, index)

    for side in range(2):
        row = LO if side == 0 else HI - 1
        for k in range(6):
            bs[side, k : k + 1, :] = strip_row(Y_SET[side][k])[row : row + 1, :]
    y_first = [along_y(side, bs.at[side], br.at[side], side) for side in range(2)]
    for copy in y_first:
        copy.start()
    far_fill(False)
    for copy in far_y + x_copies:
        copy.wait_recv()
    for side in range(2):
        row = HI if side == 0 else LO - 1
        for k in range(6):
            member = Y_SET[side][k]
            for xs, start in ((0, 10), (1, 0)):
                value = ye[2 * side + xs, 2 * k : 2 * k + 2, :]
                if member == PSI:
                    ps[start : start + 2, row, :] = value
                else:
                    pg[SLOT[member], start : start + 2, row, :] = value
    for xi, slot in ((0, RHO2), (1, RHO2), (10, RHO), (11, RHO)):
        value = pg[slot, xi, LO:HI, :]
        density[xi] = value
        ps[xi, LO:HI, :] = 1.0 - jnp.exp(-value)
    lax.fori_loop(1, 3, collide_pass, 0)
    lax.fori_loop(9, 11, collide_pass, 0)
    for copy in y_first:
        copy.wait_recv()
    for side in range(2):
        row = HI if side == 0 else LO - 1
        for k in range(6):
            strip_row(Y_SET[side][k])[row : row + 1, :] = br[side, k : k + 1, :]

    g = []
    for member in range(19):
        dx, dy, dz = DIRECTIONS[member]
        g.append(roll(strip[SLOT[member], LO + dy : HI + dy, :], -(16 * dz + dx)))
    psi, grad = gradient(
        lambda dx, dy: roll(sps[LO + dy : HI + dy, :], -dx), lambda value: roll(value, -16), lambda value: roll(value, 16)
    )
    inside = span(17, 10) | span(33, 10) | span(81, 10) | span(97, 10)
    own_rho = jnp.where(inside, strip[RHO, LO:HI, :], 1.0)
    force_bar, h, base, near = collide(g, own_rho, [strip[MOM + c, LO:HI, :] for c in range(3)], psi, grad)
    for c in range(3):
        fs[c, LO:HI, :] = jnp.where(inside, psi * force_bar[c], 0.0)
        so[20 + c] = h[c]
    so[19] = base - COUPLING * ((1.0 - psi) * near)
    for member in range(19):
        so[member] = (1.0 - OMEGA) * g[member]

    def patch(xi, carry):
        for c in range(3):
            outer = fs[c, LO:HI, :]
            fp[c, xi, LO:HI, :] = jnp.where(
                upper, roll(outer, 47 - xi), jnp.where(lower, roll(outer, 96 - xi), fp[c, xi, LO:HI, :])
            )
        return carry

    lax.fori_loop(1, 11, patch, 0)
    beyond = lane >= 64

    def signed(value):
        return jnp.where(beyond, value, -value)

    fx, fz = fs[0, LO:HI, :], signed(fs[2, LO:HI, :])
    rs[...] = W1 * fz + W2 * (
        roll(fx + fz, -1) - roll(fx - fz, 1)
        + (fs[1, LO + 1 : HI + 1, :] + signed(fs[2, LO + 1 : HI + 1, :]))
        - (fs[1, LO - 1 : HI - 1, :] - signed(fs[2, LO - 1 : HI - 1, :]))
    )

    sub8 = lax.broadcasted_iota(jnp.int32, (8, 128), 0)
    for side in range(2):
        sign = 1.0 if side == 0 else -1.0
        row = LO if side == 0 else HI - 1

        def column(value, start):
            picked = jnp.where(lane8 == sub8 + start, jnp.broadcast_to(value, (8, 128)), 0.0)
            return jnp.sum(picked, axis=1, keepdims=True)

        fx_p, fx_m = fp[0, 3:11, row, :], fp[0, 1:9, row, :]
        fy_p, fy_m = fp[1, 3:11, row, :], fp[1, 1:9, row, :]
        fy, fz = sign * fp[1, 2:10, row, :], fp[2, 2:10, row, :]
        sy, sz = sign * fs[1, row : row + 1, :], fs[2, row : row + 1, :]
        over = jnp.where(lane8 == 127, column(sy + sz, 98), roll(fy + fz, -1))
        under = jnp.where(lane8 == 0, column(sy - sz, 18), roll(fy - fz, 1))
        cs[side] = W1 * fy + W2 * ((fx_p - fx_m) + sign * (fy_p + fy_m) + over + under)
    y_second = [along_y(side, cs.at[side], cr.at[side], 2 + side) for side in range(2)]
    for copy in y_second:
        copy.start()

    def combined(own_parts, base, h):
        plus = [base + c for c in h]
        minus = [base - c for c in h]
        outs = []
        for member in range(19):
            total = base
            for c, o in enumerate(DIRECTIONS[member]):
                if o != 0:
                    total = (plus[c] if o > 0 else minus[c]) if total is base else (
                        total + h[c] if o > 0 else total - h[c]
                    )
            outs.append(own_parts[member] + total)
        return outs

    for member, value in enumerate(combined([so[k] for k in range(19)], so[19], [so[20 + c] for c in range(3)])):
        so[member] = value

    def spread_pass(x, carry):
        xi = x + 2

        def cell(c, dx, dy):
            return fp[c, xi + dx, LO + dy : HI + dy, :]

        q = cell(0, 1, 0) - cell(0, -1, 0) + cell(1, 0, 1) - cell(1, 0, -1)
        r = cell(2, 1, 0) + cell(2, -1, 0) + cell(2, 0, 1) + cell(2, 0, -1)
        r = W1 * cell(2, 0, 0) + W2 * r
        corner = (
            (cell(0, 1, 1) + cell(1, 1, 1))
            - (cell(0, -1, -1) + cell(1, -1, -1))
            + (cell(0, 1, -1) - cell(1, 1, -1))
            - (cell(0, -1, 1) - cell(1, -1, 1))
        )
        q2 = W2 * q
        outer = rs[...]
        over = jnp.where(upper, roll(outer, 31 - xi), roll(q2 + r, -1))
        under = jnp.where(lower, roll(outer, 112 - xi), roll(q2 - r, 1))
        rl[x] = W1 * q + W2 * corner + over + under
        outs = combined([hs[4 + member, xi] for member in range(19)], hs[0, xi], [hs[1 + c, xi] for c in range(3)])
        for member in range(19):
            face = so[member]
            part_ref[member, x] = jnp.where(
                upper, roll(face, 47 - xi), jnp.where(lower, roll(face, 96 - xi), outs[member])
            )
        return carry

    lax.fori_loop(0, 8, spread_pass, 0)

    for copy in z_copies + y_copies + x_copies + y_first:
        copy.wait_send()
    for copy in y_second:
        copy.wait_recv()
    rl[:, 15, :] = rl[:, 15, :] + cr[0]
    rl[:, 0, :] = rl[:, 0, :] + cr[1]
    term_ref[...] = COUPLING * dec[...] * rl[...]
    for copy in y_second:
        copy.wait_send()


def per_device(populations, adjoint_next):
    f32 = jnp.float32
    dma = pltpu.SemaphoreType.DMA
    shapes = (
        (19, 8, 16, 128),
        (24, 12, 32, 128),
        (12, 32, 128),
        (12, 16, 128),
        (8, 16, 128),
        (4, 16, 128),
        (2, 3, 8, 128),
        (2, 2, 8, 128),
        (2, 3, 8, 128),
        (4, 8, 128),
        (2, 2, 8, 128),
        (12, 16, 128),
        (24, 32, 128),
        (32, 128),
        (23, 16, 128),
        (3, 32, 128),
        (16, 128),
        (3, 12, 32, 128),
        (23, 12, 16, 128),
        (8, 16, 128),
        (2, 6, 8, 128),
        (2, 6, 8, 128),
        (4, 16, 128),
        (4, 16, 128),
        (2, 8, 128),
        (2, 8, 128),
        (2, 8, 128),
        (2, 8, 128),
    )
    part, term = pl.pallas_call(
        kernel,
        out_shape=[jax.ShapeDtypeStruct((19, 8, 16, 128), f32), jax.ShapeDtypeStruct((8, 16, 128), f32)],
        in_specs=[pl.BlockSpec(memory_space=pl.ANY)] * 2,
        out_specs=[pl.BlockSpec(memory_space=pltpu.VMEM)] * 2,
        scratch_shapes=[pltpu.VMEM(shape, f32) for shape in shapes]
        + [pltpu.SemaphoreType.REGULAR((14,)), dma((19,)), dma((19,)), dma((18,)), dma((18,)), dma((4,)), dma((4,))],
        compiler_params=pltpu.CompilerParams(
            collective_id=0, has_side_effects=True, vmem_limit_bytes=40 * 1024 * 1024
        ),
    )(
        pltpu.with_memory_space_constraint(populations, pltpu.HBM),
        pltpu.with_memory_space_constraint(adjoint_next, pltpu.HBM),
    )
    return part + term[None]


def solution(mesh):
    return jax.shard_map(
        per_device,
        mesh=mesh,
        in_specs=(P(None, "gx", "gy", "gz"), P(None, "gx", "gy", "gz")),
        out_specs=P(None, "gx", "gy", "gz"),
        check_vma=False,
    )
```

```python
import jax
import jax.numpy as jnp
from jax import lax
from jax.experimental import pallas as pl
from jax.experimental.pallas import tpu as pltpu
from jax.sharding import PartitionSpec as P

DIRECTIONS = (
    (0, 0, 0),
    (1, 0, 0),
    (-1, 0, 0),
    (0, 1, 0),
    (0, -1, 0),
    (0, 0, 1),
    (0, 0, -1),
    (1, 1, 0),
    (-1, -1, 0),
    (1, -1, 0),
    (-1, 1, 0),
    (1, 0, 1),
    (-1, 0, -1),
    (1, 0, -1),
    (-1, 0, 1),
    (0, 1, 1),
    (0, -1, -1),
    (0, 1, -1),
    (0, -1, 1),
)
W0, W1, W2 = 1.0 / 3.0, 1.0 / 18.0, 1.0 / 36.0
OMEGA = 1.0 / 0.8
KAPPA = 1.0 - 0.5 / 0.8
COUPLING = -5.5

X_PLUS = (1, 7, 9, 11, 13)
X_ZERO = (0, 3, 4, 5, 6, 15, 16, 17, 18)
X_MINUS = (2, 8, 10, 12, 14)
RHO, MOM, RHO2 = 5, 6, 18
SLOT = {}
for place, member in enumerate(X_PLUS):
    SLOT[member] = place
for place, member in enumerate(X_ZERO):
    SLOT[member] = 9 + place
for place, member in enumerate(X_MINUS):
    SLOT[member] = 19 + place
PSI = -1
Y_SET = ((3, 15, 17, 7, PSI, 10), (4, 16, 18, 9, PSI, 8))
UP = (5, 11, 14, 15, 18)
DOWN = (6, 13, 12, 17, 16)
FLAT = (0, 1, 2, 3, 4, 7, 8, 9, 10)
QUAD = (0, 1, 4, 5, 8, 9)
LO, HI = 8, 24
MESH_ID = pl.DeviceIdType.MESH
NEAR = (
    (0, 0, 1), (0, 0, -1), (1, 0, 1), (1, 0, -1), (-1, 0, 1), (-1, 0, -1),
    (1, 1, 0), (1, -1, 0), (-1, 1, 0), (-1, -1, 0), (0, 1, 0), (0, -1, 0), (1, 0, 0), (-1, 0, 0),
)


def roll(value, amount, axis=1):
    if isinstance(amount, int):
        amount = amount % value.shape[axis]
        if amount == 0:
            return value
    return pltpu.roll(value, amount, axis)


def collide(g, rho, mom, psi, grad):
    s = {i: g[i] + g[i + 1] for i in range(1, 19, 2)}
    d = {i: g[i] - g[i + 1] for i in range(1, 19, 2)}
    sxy, sxz, syz = s[7] + s[9], s[11] + s[13], s[15] + s[17]
    a = W0 * g[0] + W1 * (s[1] + s[3] + s[5]) + W2 * (sxy + sxz + syz)
    b = (
        3.0 * W1 * d[1] + 3.0 * W2 * ((d[7] + d[9]) + (d[11] + d[13])),
        3.0 * W1 * d[3] + 3.0 * W2 * ((d[7] - d[9]) + (d[15] + d[17])),
        3.0 * W1 * d[5] + 3.0 * W2 * ((d[11] - d[13]) + (d[15] - d[17])),
    )
    a3 = 3.0 * a
    txx = 9.0 * W1 * s[1] + 9.0 * W2 * (sxy + sxz) - a3
    tyy = 9.0 * W1 * s[3] + 9.0 * W2 * (sxy + syz) - a3
    tzz = 9.0 * W1 * s[5] + 9.0 * W2 * (sxz + syz) - a3
    txy = 9.0 * W2 * (s[7] - s[9])
    txz = 9.0 * W2 * (s[11] - s[13])
    tyz = 9.0 * W2 * (s[15] - s[17])
    inverse = 1.0 / rho
    strength = -COUPLING * psi
    force = [strength * c for c in grad]
    u = [(mom[c] + 0.5 * force[c]) * inverse for c in range(3)]
    accel = [c * inverse for c in force]

    def tensor(v):
        return (
            txx * v[0] + txy * v[1] + txz * v[2],
            txy * v[0] + tyy * v[1] + tyz * v[2],
            txz * v[0] + tyz * v[1] + tzz * v[2],
        )

    tu, w = tensor(u), tensor(accel)
    v = [b[c] + tu[c] for c in range(3)]
    force_bar = [v[c] + (0.5 * KAPPA) * w[c] for c in range(3)]
    h = [OMEGA * v[c] + KAPPA * w[c] for c in range(3)]
    e = a + 0.5 * (u[0] * (b[0] + v[0]) + u[1] * (b[1] + v[1]) + u[2] * (b[2] + v[2]))
    near = force_bar[0] * grad[0] + force_bar[1] * grad[1] + force_bar[2] * grad[2]
    base = OMEGA * e - (u[0] * h[0] + u[1] * h[1] + u[2] * h[2])
    return force_bar, h, base, near


def gradient(get, up, down):
    psi = get(0, 0)
    xp, xm, yp, ym = get(1, 0), get(-1, 0), get(0, 1), get(0, -1)
    along_x, along_y = xp - xm, yp - ym
    along_z = W1 * psi + W2 * (xp + xm + yp + ym)
    main, cross = get(1, 1) - get(-1, -1), get(1, -1) - get(-1, 1)
    grad = (
        W1 * along_x + W2 * ((main + cross) + (up(along_x) + down(along_x))),
        W1 * along_y + W2 * ((main - cross) + (up(along_y) + down(along_y))),
        up(along_z) - down(along_z),
    )
    return psi, grad


def kernel(pop_hbm, adj_hbm, part_ref, term_ref,
           pops, pg, ps, density, dec, zt, zf, ze, rf, re, ro, zz, strip, sps, so, fs, rs, fp, hs, rl,
           ys, yr, ye, yx, bs, br, cs, cr,
           ready, sem_pop, sem_adj, send, recv, send_y, recv_y):
    sizes = [lax.axis_size(name) for name in ("gx", "gy", "gz")]
    here = [lax.axis_index(name) for name in ("gx", "gy", "gz")]

    def at(offset):
        return tuple(lax.rem(h + o + n, n) for h, o, n in zip(here, offset, sizes))

    def ages(offset):
        (px, _, pz), (x, _, z) = at(offset), here
        half = sizes[2] // 2
        low, other_low = (z < half).astype(jnp.int32), (pz < half).astype(jnp.int32)
        wrap = (jnp.abs(px - x) > 1).astype(jnp.int32) * (low == other_low).astype(jnp.int32)
        other = other_low * (1 - low) + wrap * (px == 0).astype(jnp.int32)
        own = low * (1 - other_low) + wrap * (x == 0).astype(jnp.int32)
        return other, own

    def opposite(offset):
        return tuple(-o for o in offset)

    barrier = pltpu.get_barrier_semaphore()
    expected = 0
    for offset in NEAR:
        other_elder, own_elder = ages(offset)
        expected = expected + (1 - own_elder)

        @pl.when(other_elder == 0)
        def _():
            pl.semaphore_signal(barrier, inc=1, device_id=at(offset), device_id_type=MESH_ID)

    own = pl.ds(2, 8)
    pop_in = [
        pltpu.make_async_copy(pop_hbm.at[pl.ds(i, n)], pops.at[pl.ds(i, n)], sem_pop.at[i])
        for i, n in ((0, 5), (5, 5), (10, 5), (15, 4))
    ]
    adj_in = [
        pltpu.make_async_copy(
            adj_hbm.at[pl.ds(i, n)], pg.at[pl.ds(SLOT[i], n), own, pl.ds(LO, 16), :], sem_adj.at[i]
        )
        for i, n in ((0, 1), (1, 1), (2, 1), (3, 4), (7, 1), (8, 1), (9, 1), (10, 1), (11, 1), (12, 1), (13, 1), (14, 1), (15, 4))
    ]
    for copy in pop_in + adj_in:
        copy.start()
    pl.semaphore_wait(barrier, expected)
    for index, offset in enumerate(NEAR):
        other_elder, _ = ages(offset)

        @pl.when(other_elder == 1)
        def _():
            pl.semaphore_signal(ready.at[index], inc=1, device_id=at(offset), device_id_type=MESH_ID)

    lane = lax.broadcasted_iota(jnp.int32, (16, 128), 1)
    lane8 = lane[:8]
    upper, lower = lane == 127, lane == 0
    for ref in (sps, fs, strip, fp):
        ref[...] = jnp.zeros(ref.shape, jnp.float32)
    for copy in pop_in:
        copy.wait()

    def density_pass(x, carry):
        f = [pops[i, x] for i in range(19)]
        rho = f[0]
        for i in range(1, 19):
            rho = rho + f[i]
        decay = jnp.exp(-rho)
        pg[RHO, x + 2, LO:HI, :] = rho
        pg[RHO2, x + 2, LO:HI, :] = rho
        density[x + 2] = rho
        dec[x] = decay
        ps[x + 2, LO:HI, :] = 1.0 - decay
        d = {i: f[i] - f[i + 1] for i in range(1, 19, 2)}
        pg[MOM, x + 2, LO:HI, :] = d[1] + (d[7] + d[9]) + (d[11] + d[13])
        pg[MOM + 1, x + 2, LO:HI, :] = d[3] + (d[7] - d[9]) + (d[15] + d[17])
        pg[MOM + 2, x + 2, LO:HI, :] = d[5] + (d[11] - d[13]) + (d[15] - d[17])
        return carry

    lax.fori_loop(0, 8, density_pass, 0)
    for copy in adj_in:
        copy.wait()

    def pack(x, carry):
        up_a, up_b, low_q, low_a, low_b = carry

        def split(j):
            if j == 5:
                return pg[RHO, x + 2, LO:HI, :]
            return jnp.where(lane < 64, pg[SLOT[UP[j]], x + 2, LO:HI, :], pg[SLOT[DOWN[j]], x + 2, LO:HI, :])

        for j in range(6):
            value = split(j)
            for deeper in range(2):
                target = 8 * (QUAD[j] + 2 * deeper) + x
                moved = roll(value, lax.rem(target + 128 - deeper, 128))
                up_a = jnp.where(lane == target, moved, up_a)
                low_q = jnp.where(lane == lax.rem(target + 126, 128), moved, low_q)
        for j in range(12):
            value = pg[SLOT[FLAT[j]], x + 2, LO:HI, :] if j < 9 else pg[MOM + j - 9, x + 2, LO:HI, :]
            target = 8 * ((12 + j) % 16) + x
            moved = roll(value, target)
            mark, low_mark = lane == target, lane == lax.rem(target + 127, 128)
            if j < 4:
                up_a = jnp.where(mark, moved, up_a)
                low_a = jnp.where(low_mark, moved, low_a)
            else:
                up_b = jnp.where(mark, moved, up_b)
                low_b = jnp.where(low_mark, moved, low_b)
        return up_a, up_b, low_q, low_a, low_b

    nothing = jnp.zeros((16, 128), jnp.float32)
    up_a, up_b, low_q, low_a, low_b = lax.fori_loop(0, 8, pack, (nothing,) * 5)
    low_a = jnp.where(lane < 96, roll(low_q, 2), roll(low_a, 1))
    low_b = roll(low_b, 1)
    in_eight = lax.rem(lane, 8)
    for side, (a, b) in enumerate(((up_a, up_b), (low_a, low_b))):
        zt[2 * side] = a
        zt[2 * side + 1] = b
        edge = jnp.where(
            (in_eight < 2) | (in_eight >= 6), a, jnp.where(in_eight < 4, roll(b, 2), roll(b, -2))
        )
        zf[side, 0] = a[:8]
        zf[side, 1] = a[8:]
        zf[side, 2] = jnp.where(lane8 < 64, b[:8], roll(b[8:], 64))
        ze[0, side] = jnp.where(in_eight[:8] < 4, edge[:8], roll(edge[8:], 4))
        ze[1, side] = jnp.where(in_eight[:8] >= 4, edge[:8], roll(edge[8:], -4))

    for side in range(2):
        row = LO if side == 0 else HI - 1
        for k in range(6):
            member = Y_SET[side][k]
            ys[side, k] = ps[2:10, row, :] if member == PSI else pg[SLOT[member], 2:10, row, :]
    for side in range(2):
        for xs in range(2):
            for k in range(6):
                yx[2 * side + xs, 2 * k : 2 * k + 2, :] = ys[side, k, 6 * xs : 6 * xs + 2, :]
    def copy_to(offset, src, dst, sends, recvs, index):
        return pltpu.make_async_remote_copy(
            src_ref=src, dst_ref=dst, send_sem=sends.at[index], recv_sem=recvs.at[index],
            device_id=at(tuple(-o for o in offset)), device_id_type=MESH_ID,
        )

    def message(index, offset, src, dst):
        copy = copy_to(offset, src, dst, send, recv, index)
        by_offset[offset].append(copy)
        return copy

    z_copies, y_copies, x_copies = [], [], []
    by_offset = {offset: [] for offset in NEAR}
    block = pl.ds(LO, 16)
    for offset in NEAR:
        dx, dy, dz = offset
        if dz != 0:
            side = 0 if dz > 0 else 1
            if dx == 0:
                z_copies.append(message(side, offset, zf.at[side], rf.at[side]))
            else:
                xs = 0 if dx > 0 else 1
                z_copies.append(
                    message(2 + 2 * side + xs, offset, ze.at[xs, side], re.at[2 * side + xs])
                )
    for xs in range(2):
        offset = (1 - 2 * xs, 0, 0)
        z_copies.append(message(6 + xs, offset, ze.at[xs], ro.at[xs]))
    for side in range(2):
        for xs in range(2):
            offset = (1 - 2 * xs, 1 - 2 * side, 0)
            y_copies.append(message(8 + 2 * side + xs, offset, yx.at[2 * side + xs], ye.at[2 * side + xs]))
        y_copies.append(message(12 + side, (0, 1 - 2 * side, 0), ys.at[side], yr.at[side]))
    for xs in range(2):
        offset = (1 - 2 * xs, 0, 0)
        if xs == 0:
            parts = ((pl.ds(0, 18), 2, 10), (pl.ds(0, 6), 3, 11))
        else:
            parts = ((pl.ds(6, 18), 9, 1), (pl.ds(18, 6), 8, 0))
        for k, (slots, near, far) in enumerate(parts):
            x_copies.append(
                message(14 + 2 * xs + k, offset, pg.at[slots, near, block, :], pg.at[slots, far, block, :])
            )
    for offset in NEAR:
        _, own_elder = ages(opposite(offset))

        @pl.when(own_elder == 0)
        def _():
            for copy in by_offset[offset]:
                copy.start()


    def span(start, count):
        return (lane >= start) & (lane < start + count)

    def place(value, tile, source, group, start, count, deep):
        mark = span(16 * group + start, count)
        if deep:
            mark = mark | span(16 * group + 16 + start, count)
        return jnp.where(mark, roll(tile, 16 * group + start - source), value)

    def fill(value, tiles, side, spot, group, deep):
        return place(value, tiles[2 * side + spot // 16], 8 * (spot % 16), group, 2, 8, deep)

    def fill_edges(value, own, side, spot, group, deep, cx):
        for xs, start, low, high in ((0, 10, 0, 2), (1, 0, 6, 4)):
            if cx is not None and cx == (-1 if xs == 0 else 1):
                continue
            tile = zz[8 + 2 * xs + side] if own else zz[4 + 2 * side + xs]
            source = 8 * (spot % 16) + (low if spot < 16 else high)
            value = place(value, tile, source, group, start, 2, deep)
        return value

    parts = []
    for j in range(5):
        parts.append((SLOT[UP[j]], DIRECTIONS[UP[j]][0], [(True, 0, QUAD[j], 2, True), (False, 0, QUAD[j], 6, True)]))
        parts.append((SLOT[DOWN[j]], DIRECTIONS[DOWN[j]][0], [(True, 1, QUAD[j], 4, True), (False, 1, QUAD[j], 0, True)]))
    for j in range(12):
        slot, cx = (SLOT[FLAT[j]], DIRECTIONS[FLAT[j]][0]) if j < 9 else (MOM + j - 9, None)
        parts.append((slot, cx, [
            (True, 0, 12 + j, 2, False), (True, 1, 12 + j, 5, False),
            (False, 0, 12 + j, 6, False), (False, 1, 12 + j, 1, False),
        ]))
    parts.append((RHO, None, [
        (True, 0, QUAD[5], 2, True), (True, 1, QUAD[5], 4, True),
        (False, 0, QUAD[5], 6, True), (False, 1, QUAD[5], 0, True),
    ]))

    for slot, _, pieces in parts:
        value = nothing
        for own_part, side, spot, group, deep in pieces:
            if own_part:
                value = fill(value, zt, side, spot, group, deep)
        strip[slot, LO:HI, :] = value

    def collide_pass(xi, carry):
        g = []
        for member in range(19):
            dx, dy, dz = DIRECTIONS[member]
            value = roll(pg[SLOT[member], xi + dx, LO + dy : HI + dy, :], -dz)
            g.append(value)
            hs[4 + member, xi] = (1.0 - OMEGA) * value
        psi, grad = gradient(
            lambda dx, dy: ps[xi + dx, LO + dy : HI + dy, :], lambda value: roll(value, -1), lambda value: roll(value, 1)
        )
        force_bar, h, base, near = collide(
            g, density[xi], [pg[MOM + c, xi, LO:HI, :] for c in range(3)], psi, grad
        )
        for c in range(3):
            fp[c, xi, LO:HI, :] = psi * force_bar[c]
            hs[1 + c, xi] = h[c]
        hs[0, xi] = base - COUPLING * ((1.0 - psi) * near)
        return carry

    near_y = y_copies[2::3]
    far_y = [copy for copy in y_copies if not any(copy is other for other in near_y)]
    for copy in near_y:
        copy.wait_recv()
    for side in range(2):
        row = HI if side == 0 else LO - 1
        for k in range(6):
            member = Y_SET[side][k]
            for start, count, value in ((2, 8, yr[side, k]),):
                if member == PSI:
                    ps[start : start + count, row, :] = value
                else:
                    pg[SLOT[member], start : start + count, row, :] = value
    lax.fori_loop(3, 9, collide_pass, 0)
    for index, offset in reversed(tuple(enumerate(NEAR))):
        _, own_elder = ages(opposite(offset))

        @pl.when(own_elder == 1)
        def _():
            pl.semaphore_wait(ready.at[index], 1)
            for copy in by_offset[offset]:
                copy.start()

    for copy in z_copies:
        copy.wait_recv()
    for side in range(2):
        zz[2 * side, 0:8, :] = rf[side, 0]
        zz[2 * side, 8:16, :] = rf[side, 1]
        zz[2 * side + 1, 0:8, :] = rf[side, 2]
        zz[2 * side + 1, 8:16, :] = roll(rf[side, 2], 64)
        for xs in range(2):
            for target, tile in ((4 + 2 * side + xs, re[2 * side + xs]), (8 + 2 * xs + side, ro[xs, side])):
                zz[target, 0:8, :] = tile
                zz[target, 8:16, :] = roll(tile, -4 if xs == 0 else 4)
    def far_fill(wanted):
        for slot, cx, pieces in parts:
            if wanted != (slot in urgent):
                continue
            value = strip[slot, LO:HI, :]
            for own_part, side, spot, group, deep in pieces:
                if not own_part:
                    value = fill(value, zz, side, spot, group, deep)
                value = fill_edges(value, own_part, side, spot, group, deep, cx)
            strip[slot, LO:HI, :] = value

    urgent = {RHO} | {SLOT[member] for side in range(2) for member in Y_SET[side] if member != PSI}
    far_fill(True)
    sps[LO:HI, :] = 1.0 - jnp.exp(-strip[RHO, LO:HI, :])

    def strip_row(member):
        return sps if member == PSI else strip.at[SLOT[member]]

    def along_y(side, src, dst, index):
        return copy_to((0, 1 - 2 * side, 0), src, dst, send_y, recv_y, index)

    for side in range(2):
        row = LO if side == 0 else HI - 1
        for k in range(6):
            bs[side, k : k + 1, :] = strip_row(Y_SET[side][k])[row : row + 1, :]
    y_first = [along_y(side, bs.at[side], br.at[side], side) for side in range(2)]
    for copy in y_first:
        copy.start()
    far_fill(False)
    for copy in far_y + x_copies:
        copy.wait_recv()
    for side in range(2):
        row = HI if side == 0 else LO - 1
        for k in range(6):
            member = Y_SET[side][k]
            for xs, start in ((0, 10), (1, 0)):
                value = ye[2 * side + xs, 2 * k : 2 * k + 2, :]
                if member == PSI:
                    ps[start : start + 2, row, :] = value
                else:
                    pg[SLOT[member], start : start + 2, row, :] = value
    for xi, slot in ((0, RHO2), (1, RHO2), (10, RHO), (11, RHO)):
        value = pg[slot, xi, LO:HI, :]
        density[xi] = value
        ps[xi, LO:HI, :] = 1.0 - jnp.exp(-value)
    lax.fori_loop(1, 3, collide_pass, 0)
    lax.fori_loop(9, 11, collide_pass, 0)
    for copy in y_first:
        copy.wait_recv()
    for side in range(2):
        row = HI if side == 0 else LO - 1
        for k in range(6):
            strip_row(Y_SET[side][k])[row : row + 1, :] = br[side, k : k + 1, :]

    g = []
    for member in range(19):
        dx, dy, dz = DIRECTIONS[member]
        g.append(roll(strip[SLOT[member], LO + dy : HI + dy, :], -(16 * dz + dx)))
    psi, grad = gradient(
        lambda dx, dy: roll(sps[LO + dy : HI + dy, :], -dx), lambda value: roll(value, -16), lambda value: roll(value, 16)
    )
    inside = span(17, 10) | span(33, 10) | span(81, 10) | span(97, 10)
    own_rho = jnp.where(inside, strip[RHO, LO:HI, :], 1.0)
    force_bar, h, base, near = collide(g, own_rho, [strip[MOM + c, LO:HI, :] for c in range(3)], psi, grad)
    for c in range(3):
        fs[c, LO:HI, :] = jnp.where(inside, psi * force_bar[c], 0.0)
        so[20 + c] = h[c]
    so[19] = base - COUPLING * ((1.0 - psi) * near)
    for member in range(19):
        so[member] = (1.0 - OMEGA) * g[member]

    def patch(xi, carry):
        for c in range(3):
            outer = fs[c, LO:HI, :]
            fp[c, xi, LO:HI, :] = jnp.where(
                upper, roll(outer, 47 - xi), jnp.where(lower, roll(outer, 96 - xi), fp[c, xi, LO:HI, :])
            )
        return carry

    lax.fori_loop(1, 11, patch, 0)
    beyond = lane >= 64

    def signed(value):
        return jnp.where(beyond, value, -value)

    fx, fz = fs[0, LO:HI, :], signed(fs[2, LO:HI, :])
    rs[...] = W1 * fz + W2 * (
        roll(fx + fz, -1) - roll(fx - fz, 1)
        + (fs[1, LO + 1 : HI + 1, :] + signed(fs[2, LO + 1 : HI + 1, :]))
        - (fs[1, LO - 1 : HI - 1, :] - signed(fs[2, LO - 1 : HI - 1, :]))
    )

    sub8 = lax.broadcasted_iota(jnp.int32, (8, 128), 0)
    for side in range(2):
        sign = 1.0 if side == 0 else -1.0
        row = LO if side == 0 else HI - 1

        def column(value, start):
            picked = jnp.where(lane8 == sub8 + start, jnp.broadcast_to(value, (8, 128)), 0.0)
            return jnp.sum(picked, axis=1, keepdims=True)

        fx_p, fx_m = fp[0, 3:11, row, :], fp[0, 1:9, row, :]
        fy_p, fy_m = fp[1, 3:11, row, :], fp[1, 1:9, row, :]
        fy, fz = sign * fp[1, 2:10, row, :], fp[2, 2:10, row, :]
        sy, sz = sign * fs[1, row : row + 1, :], fs[2, row : row + 1, :]
        over = jnp.where(lane8 == 127, column(sy + sz, 98), roll(fy + fz, -1))
        under = jnp.where(lane8 == 0, column(sy - sz, 18), roll(fy - fz, 1))
        cs[side] = W1 * fy + W2 * ((fx_p - fx_m) + sign * (fy_p + fy_m) + over + under)
    y_second = [along_y(side, cs.at[side], cr.at[side], 2 + side) for side in range(2)]
    for copy in y_second:
        copy.start()

    def combined(own_parts, base, h):
        plus = [base + c for c in h]
        minus = [base - c for c in h]
        outs = []
        for member in range(19):
            total = base
            for c, o in enumerate(DIRECTIONS[member]):
                if o != 0:
                    total = (plus[c] if o > 0 else minus[c]) if total is base else (
                        total + h[c] if o > 0 else total - h[c]
                    )
            outs.append(own_parts[member] + total)
        return outs

    for member, value in enumerate(combined([so[k] for k in range(19)], so[19], [so[20 + c] for c in range(3)])):
        so[member] = value

    def spread_pass(x, carry):
        xi = x + 2

        def cell(c, dx, dy):
            return fp[c, xi + dx, LO + dy : HI + dy, :]

        q = cell(0, 1, 0) - cell(0, -1, 0) + cell(1, 0, 1) - cell(1, 0, -1)
        r = cell(2, 1, 0) + cell(2, -1, 0) + cell(2, 0, 1) + cell(2, 0, -1)
        r = W1 * cell(2, 0, 0) + W2 * r
        corner = (
            (cell(0, 1, 1) + cell(1, 1, 1))
            - (cell(0, -1, -1) + cell(1, -1, -1))
            + (cell(0, 1, -1) - cell(1, 1, -1))
            - (cell(0, -1, 1) - cell(1, -1, 1))
        )
        q2 = W2 * q
        outer = rs[...]
        over = jnp.where(upper, roll(outer, 31 - xi), roll(q2 + r, -1))
        under = jnp.where(lower, roll(outer, 112 - xi), roll(q2 - r, 1))
        rl[x] = W1 * q + W2 * corner + over + under
        outs = combined([hs[4 + member, xi] for member in range(19)], hs[0, xi], [hs[1 + c, xi] for c in range(3)])
        for member in range(19):
            face = so[member]
            part_ref[member, x] = jnp.where(
                upper, roll(face, 47 - xi), jnp.where(lower, roll(face, 96 - xi), outs[member])
            )
        return carry

    lax.fori_loop(0, 8, spread_pass, 0)

    for copy in z_copies + y_copies + x_copies + y_first:
        copy.wait_send()
    for copy in y_second:
        copy.wait_recv()
    rl[:, 15, :] = rl[:, 15, :] + cr[0]
    rl[:, 0, :] = rl[:, 0, :] + cr[1]
    term_ref[...] = COUPLING * dec[...] * rl[...]
    for copy in y_second:
        copy.wait_send()


def per_device(populations, adjoint_next):
    f32 = jnp.float32
    dma = pltpu.SemaphoreType.DMA
    shapes = (
        (19, 8, 16, 128),
        (24, 12, 32, 128),
        (12, 32, 128),
        (12, 16, 128),
        (8, 16, 128),
        (4, 16, 128),
        (2, 3, 8, 128),
        (2, 2, 8, 128),
        (2, 3, 8, 128),
        (4, 8, 128),
        (2, 2, 8, 128),
        (12, 16, 128),
        (24, 32, 128),
        (32, 128),
        (23, 16, 128),
        (3, 32, 128),
        (16, 128),
        (3, 12, 32, 128),
        (23, 12, 16, 128),
        (8, 16, 128),
        (2, 6, 8, 128),
        (2, 6, 8, 128),
        (4, 16, 128),
        (4, 16, 128),
        (2, 8, 128),
        (2, 8, 128),
        (2, 8, 128),
        (2, 8, 128),
    )
    part, term = pl.pallas_call(
        kernel,
        out_shape=[jax.ShapeDtypeStruct((19, 8, 16, 128), f32), jax.ShapeDtypeStruct((8, 16, 128), f32)],
        in_specs=[pl.BlockSpec(memory_space=pl.ANY)] * 2,
        out_specs=[pl.BlockSpec(memory_space=pltpu.VMEM)] * 2,
        scratch_shapes=[pltpu.VMEM(shape, f32) for shape in shapes]
        + [pltpu.SemaphoreType.REGULAR((14,)), dma((19,)), dma((19,)), dma((18,)), dma((18,)), dma((4,)), dma((4,))],
        compiler_params=pltpu.CompilerParams(
            collective_id=0, has_side_effects=True, vmem_limit_bytes=40 * 1024 * 1024
        ),
    )(
        pltpu.with_memory_space_constraint(populations, pltpu.HBM),
        pltpu.with_memory_space_constraint(adjoint_next, pltpu.HBM),
    )
    return part + term[None]


def solution(mesh):
    return jax.shard_map(
        per_device,
        mesh=mesh,
        in_specs=(P(None, "gx", "gy", "gz"), P(None, "gx", "gy", "gz")),
        out_specs=P(None, "gx", "gy", "gz"),
        check_vma=False,
    )
```
